32 devices in a mesh: dp: 4 (over x, core), mp: 8 (over z, y).
Axes of the slice: x: 2, y: 2, z: 4, core: 2. Of those that a mesh axis runs over, the one named last changes fastest.
Arguments:
- source_prompts: bfloat16 [128, 64, 4096], P(None, None, 'mp'), may hold values from -6 to 6
- task_logits: float32 [8, 128], replicated, may hold values from -8 to 260
- task_ids: int32 [32], P('dp'), may hold values from 0 to 7
- key_weight: bfloat16 [4096, 4096], P(None, 'mp'), may hold values from -0.09375 to 0.09375
- value_weight: bfloat16 [4096, 4096], P(None, 'mp'), may hold values from -0.09375 to 0.09375
- queries: bfloat16 [32, 128, 4096], P(('dp', 'mp')), may hold values from -32 to 32
- keys: bfloat16 [32, 128, 4096], P(('dp', 'mp')), may hold values from -16 to 16
- values: bfloat16 [32, 128, 4096], P(('dp', 'mp')), may hold values from -6 to 6
- cotangent: bfloat16 [32, 128, 4096], P(('dp', 'mp')), may hold values from -6 to 6
Outputs:
- attended: bfloat16 [32, 128, 4096], P(('dp', 'mp'))
- source_grad: float32 [128, 64, 4096], P(None, 'dp', 'mp')
- logits_grad: float32 [8, 128], replicated
The draws below stay inside these ranges and needn't reach their ends.
All inputs are finite; a program needn't handle non-finite values.
Results may differ from the reference program's by a relative error of at most 0.011.
Values may be sent and summed in bfloat16 or wider, within the bound.
A program may use at most 128 MiB of HBM per device.

```python
import jax
import jax.numpy as jnp
from jax import lax

D = 4096
HEADS = 32
DH = 128
NSRC = 128
NTASK = 8
PTOK = 64
SEQ = 128
EXAMPLES = 32


def query_key_pair(key):
    paired_key = jax.random.fold_in(key, 11)
    query_seed, key_seed = jax.random.split(paired_key, 2)
    full_shape = (EXAMPLES, SEQ, D)
    query_draw = jax.random.normal(query_seed, full_shape, jnp.float32)
    key_draw = jax.random.normal(key_seed, full_shape, jnp.float32)
    return (jnp.clip(query_draw, -32.0, 32.0), jnp.clip(key_draw, -16.0, 16.0))


def draw_queries(key, part):
    return query_key_pair(key)[0].astype(jnp.bfloat16)


def draw_keys(key, part):
    return query_key_pair(key)[1].astype(jnp.bfloat16)


def draw_task_logits(key, part):
    logit_key = jax.random.fold_in(key, 23)
    base_seed = jax.random.fold_in(logit_key, 0)
    logits = jnp.clip(2.0 * jax.random.normal(base_seed, (NTASK, NSRC), jnp.float32), -8.0, 8.0)
    return logits


def plant(result, own_key, smallest, high):
    place = [jax.random.randint(jax.random.fold_in(own_key, axis), (), 0, length) for axis, length in enumerate(result.shape)]
    main_axis = result.shape.index(max(result.shape))
    beside = place[:main_axis] + [(place[main_axis] + 1) % result.shape[main_axis]] + place[main_axis + 1:]
    return result.at[tuple(place)].set(smallest).at[tuple(beside)].set(high)


def steps_of(rng, extent, cuts, least, largest):
    level, own = 1.0, jax.random.fold_in(rng, 6)
    for dim, blocks in cuts:
        steps = jnp.exp(jax.random.uniform(jax.random.fold_in(own, dim), (blocks,), jnp.float32, least / len(cuts), largest / len(cuts)))
        level = level * jnp.repeat(steps, extent[dim] // blocks).reshape([-1 if axis == dim else 1 for axis in range(len(extent))])
    return level


def centred(own_key, shape, scale, limit, pieces=(), kind=jnp.bfloat16):
    loudness = steps_of(own_key, shape, pieces, -0.22, 0.18) if pieces else 1.0
    drawn = jax.random.normal(own_key, shape, jnp.float32) * scale * loudness
    return jnp.minimum(jnp.maximum(drawn, -limit), limit).astype(kind)


def setup_inputs(seed: int = 0) -> dict:
    streams_of = jax.random.split(jax.random.key(seed), 10)
    return {
        "source_prompts": centred(streams_of[0], (NSRC, PTOK, D), 1.0, 6.0, ((2, 8),)),
        "task_logits": draw_task_logits(jax.random.fold_in(streams_of[9], 71), 0),
        "task_ids": plant(jax.random.randint(streams_of[2], (EXAMPLES,), 0, NTASK), jax.random.fold_in(streams_of[2], 1), 0, NTASK - 1).astype(jnp.int32),
        "key_weight": centred(streams_of[3], (D, D), D ** -0.5, 0.09375, ((1, 8),)),
        "value_weight": centred(streams_of[4], (D, D), D ** -0.5, 0.09375, ((1, 8),)),
        "queries": draw_queries(jax.random.fold_in(streams_of[9], 71), 0),
        "keys": draw_keys(jax.random.fold_in(streams_of[9], 71), 0),
        "values": centred(streams_of[7], (EXAMPLES, SEQ, D), 1.0, 6.0, ((0, 32),)),
        "cotangent": centred(streams_of[8], (EXAMPLES, SEQ, D), 1.0, 6.0, ((0, 32),)),
    }


mask_fill = -1.0e30


def example_pass(prompt_pair, query_rows, key_rows, value_rows, cot_rows):
    score_scale = DH ** -0.5
    key_all = jnp.concatenate([prompt_pair[:, 0, :], key_rows], axis=0)
    value_all = jnp.concatenate([prompt_pair[:, 1, :], value_rows], axis=0)
    query_heads = query_rows.astype(jnp.float32).reshape(SEQ, HEADS, DH)
    key_heads = key_all.astype(jnp.float32).reshape(PTOK + SEQ, HEADS, DH)
    value_heads = value_all.astype(jnp.float32).reshape(PTOK + SEQ, HEADS, DH)
    cot_heads = cot_rows.astype(jnp.float32).reshape(SEQ, HEADS, DH)
    scores = jnp.einsum("ihd,jhd->hij", query_heads, key_heads) * score_scale
    column = jnp.arange(PTOK + SEQ)[None, :]
    position = jnp.arange(SEQ)[:, None]
    visible = (column < PTOK) | (column - PTOK <= position)
    scores = jnp.where(visible[None], scores, mask_fill)
    top_score = jnp.max(scores, axis=2, keepdims=True)
    exponent = jnp.exp(scores - top_score)
    attention = exponent / jnp.sum(exponent, axis=2, keepdims=True)
    attention_rounded = attention.astype(jnp.bfloat16)
    attended = jnp.einsum("hij,jhd->ihd", attention_rounded.astype(jnp.float32), value_heads)
    attended = attended.astype(jnp.bfloat16).reshape(SEQ, D)
    grad_attention = jnp.einsum("ihd,jhd->hij", cot_heads, value_heads)
    inner_sum = jnp.sum(attention * grad_attention, axis=2, keepdims=True)
    grad_scores = (attention * (grad_attention - inner_sum)).astype(jnp.bfloat16)
    key_grads = jnp.einsum("hij,ihd->jhd", grad_scores[:, :, :PTOK].astype(jnp.float32), query_heads)
    key_grads = (key_grads * score_scale).astype(jnp.bfloat16)
    value_grads = jnp.einsum("hij,ihd->jhd", attention_rounded[:, :, :PTOK].astype(jnp.float32), cot_heads)
    value_grads = value_grads.astype(jnp.bfloat16)
    return attended, jnp.stack([key_grads.reshape(PTOK, D), value_grads.reshape(PTOK, D)], axis=1)


def reference(source_prompts, task_logits, task_ids, key_weight, value_weight, queries, keys, values, cotangent):
    mix_weights = jax.nn.softmax(task_logits, axis=1)
    mix_rounded = mix_weights.astype(jnp.bfloat16)
    mixture = jnp.dot(mix_rounded, source_prompts.reshape(NSRC, PTOK * D), preferred_element_type=jnp.float32)
    mixture = mixture.astype(jnp.bfloat16).reshape(NTASK * PTOK, D)
    prompt_keys = jnp.dot(mixture, key_weight, preferred_element_type=jnp.float32).astype(jnp.bfloat16)
    prompt_values = jnp.dot(mixture, value_weight, preferred_element_type=jnp.float32).astype(jnp.bfloat16)
    prompt_table = jnp.stack([prompt_keys, prompt_values], axis=1).reshape(NTASK, PTOK, 2, D)

    def one_example(packed):
        task_index, query_rows, key_rows, value_rows, cot_rows = packed
        prompt_pair = lax.dynamic_index_in_dim(prompt_table, task_index, 0, keepdims=False)
        return example_pass(prompt_pair, query_rows, key_rows, value_rows, cot_rows)

    attended, prompt_grads = lax.map(one_example, (task_ids, queries, keys, values, cotangent))
    selector = (task_ids[:, None] == jnp.arange(NTASK, dtype=jnp.int32)[None, :]).astype(jnp.float32)
    task_grads = jnp.dot(selector.T, prompt_grads.reshape(EXAMPLES, PTOK * 2 * D).astype(jnp.float32),
                         precision=lax.Precision.HIGHEST)
    task_grads = task_grads.reshape(NTASK * PTOK, 2, D)
    mixture_grad = jnp.dot(task_grads[:, 0, :], key_weight.astype(jnp.float32).T, precision=lax.Precision.HIGHEST)
    mixture_grad = mixture_grad + jnp.dot(task_grads[:, 1, :], value_weight.astype(jnp.float32).T,
                                          precision=lax.Precision.HIGHEST)
    mixture_grad = mixture_grad.reshape(NTASK, PTOK * D)
    source_grad = jnp.dot(mix_weights.T, mixture_grad, precision=lax.Precision.HIGHEST).reshape(NSRC, PTOK, D)
    weight_grad = jnp.dot(mixture_grad, source_prompts.reshape(NSRC, PTOK * D).astype(jnp.float32).T,
                          precision=lax.Precision.HIGHEST)
    logits_grad = mix_weights * (weight_grad - jnp.sum(mix_weights * weight_grad, axis=1, keepdims=True))
    return attended, source_grad, logits_grad
```

```python
import functools

import jax
import jax.numpy as jnp
from jax import lax
from jax.experimental import pallas as pl
from jax.experimental.pallas import tpu as pltpu
from jax.sharding import PartitionSpec as P

D = 4096
HEADS = 32
DH = 128
NSRC = 128
NTASK = 8
PTOK = 64
SEQ = 128
E_DEV = 1


mask_fill = -1e30


def example_block(prompt_pair, queries, keys, values, cotangent):
    examples = queries.shape[0]
    score_scale = DH ** (-0.5)
    key_all = jnp.concatenate([prompt_pair[:, :, 0, :], keys], axis=1)
    value_all = jnp.concatenate([prompt_pair[:, :, 1, :], values], axis=1)
    query_heads = queries.reshape(examples, SEQ, HEADS, DH)
    key_heads = key_all.reshape(examples, PTOK + SEQ, HEADS, DH)
    value_heads = value_all.reshape(examples, PTOK + SEQ, HEADS, DH)
    cot_heads = cotangent.reshape(examples, SEQ, HEADS, DH)
    scores = (
        jnp.einsum("eihd,ejhd->ehij", query_heads, key_heads, preferred_element_type=jnp.float32)
        * score_scale
    )
    column = jnp.arange(PTOK + SEQ)[None, :]
    position = jnp.arange(SEQ)[:, None]
    visible = (column < PTOK) | (column - PTOK <= position)
    scores = jnp.where(visible[None, None], scores, mask_fill)
    top_score = jnp.max(scores, axis=3, keepdims=True)
    exponent = jnp.exp(scores - top_score)
    attention = exponent / jnp.sum(exponent, axis=3, keepdims=True)
    attention_rounded = attention.astype(jnp.bfloat16)
    attended = jnp.einsum(
        "ehij,ejhd->eihd", attention_rounded, value_heads, preferred_element_type=jnp.float32
    )
    attended = attended.astype(jnp.bfloat16).reshape(examples, SEQ, D)
    grad_attention = jnp.einsum(
        "eihd,ejhd->ehij", cot_heads, value_heads, preferred_element_type=jnp.float32
    )
    inner_sum = jnp.sum(attention * grad_attention, axis=3, keepdims=True)
    grad_scores = (attention * (grad_attention - inner_sum)).astype(jnp.bfloat16)
    key_grads = jnp.einsum(
        "ehij,eihd->ejhd",
        grad_scores[:, :, :, :PTOK],
        query_heads,
        preferred_element_type=jnp.float32,
    )
    key_grads = (key_grads * score_scale).astype(jnp.bfloat16).reshape(examples, PTOK, D)
    value_grads = jnp.einsum(
        "ehij,eihd->ejhd",
        attention_rounded[:, :, :, :PTOK],
        cot_heads,
        preferred_element_type=jnp.float32,
    )
    value_grads = value_grads.astype(jnp.bfloat16).reshape(examples, PTOK, D)
    return (attended, jnp.stack([key_grads, value_grads], axis=2))


def tile_products(tile_grad, source_prompts, mix_weights, col_width):
    rows_here = tile_grad.shape[1]
    own_prompts = lax.dynamic_slice_in_dim(
        source_prompts, lax.axis_index("dp") * rows_here, rows_here, 1
    )
    tile_flat = tile_grad.reshape(NTASK, rows_here * col_width)
    source_grad = jnp.dot(mix_weights.T, tile_flat, precision=lax.Precision.HIGHEST)
    source_grad = source_grad.reshape(NSRC, rows_here, col_width)
    weight_part = jnp.dot(
        tile_flat,
        own_prompts.reshape(NSRC, rows_here * col_width).astype(jnp.float32).T,
        precision=lax.Precision.HIGHEST,
    )
    return (source_grad, weight_part)


def on_device(
    source_prompts,
    task_logits,
    task_ids,
    key_weight,
    value_weight,
    queries,
    keys,
    values,
    cotangent,
):
    col_width = key_weight.shape[1]
    group_examples = task_ids.shape[0]
    mix_weights = jax.nn.softmax(task_logits, axis=1)
    mix_rounded = mix_weights.astype(jnp.bfloat16)
    mixture = jnp.dot(
        mix_rounded,
        source_prompts.reshape(NSRC, PTOK * col_width),
        preferred_element_type=jnp.float32,
    )
    mixture = mixture.astype(jnp.bfloat16).reshape(NTASK, PTOK, col_width)
    pair_weight = jnp.concatenate([key_weight, value_weight], axis=1)
    portion = lax.all_gather(mixture, "mp", axis=2, tiled=True)
    portion_rows = portion.reshape(NTASK * PTOK, portion.shape[2])
    projected = jnp.dot(portion_rows, pair_weight, preferred_element_type=jnp.float32)
    projected = projected.astype(jnp.bfloat16).reshape(NTASK, PTOK, 2, col_width)
    task_range = jnp.arange(NTASK, dtype=jnp.int32)
    selector_all = (task_ids[:, None] == task_range[None, :]).astype(jnp.bfloat16)
    table_full = lax.all_gather(projected, "mp", axis=3, tiled=True)
    own_offset = lax.axis_index("mp") * E_DEV
    own_selector = lax.dynamic_slice_in_dim(selector_all, own_offset, E_DEV, 0)
    chosen = jnp.dot(
        own_selector, table_full.reshape(NTASK, PTOK * 2 * D), preferred_element_type=jnp.float32
    )
    prompt_pair = chosen.astype(jnp.bfloat16).reshape(E_DEV, PTOK, 2, D)
    attended, outgoing_grads = example_block(prompt_pair, queries, keys, values, cotangent)
    incoming = lax.all_to_all(outgoing_grads, "mp", split_axis=3, concat_axis=0, tiled=True)
    group_grads = jnp.dot(
        selector_all.T,
        incoming.reshape(group_examples, PTOK * 2 * col_width),
        preferred_element_type=jnp.float32,
    )
    pair_weight_t = pair_weight.astype(jnp.float32).T
    task_rows = lax.psum_scatter(
        group_grads.reshape(NTASK, PTOK, 2 * col_width), "dp", scatter_dimension=1, tiled=True
    )
    rows_here = task_rows.shape[1]
    row_terms = jnp.dot(
        task_rows.reshape(NTASK * rows_here, 2 * col_width),
        pair_weight_t,
        precision=lax.Precision.HIGHEST,
    ).reshape(NTASK, rows_here, D)
    tile_grad = lax.psum_scatter(row_terms, "mp", scatter_dimension=2, tiled=True)
    source_grad, weight_part = tile_products(tile_grad, source_prompts, mix_weights, col_width)
    weight_grad = lax.psum(weight_part, ("dp", "mp"))
    logits_grad = mix_weights * (
        weight_grad - jnp.sum(mix_weights * weight_grad, axis=1, keepdims=True)
    )
    return (attended, source_grad, logits_grad)


BF = jnp.bfloat16
F32 = jnp.float32


def mm(a, b, ca=1, cb=0, precision=None):
    return lax.dot_general(
        a, b, (((ca,), (cb,)), ((), ())), preferred_element_type=F32, precision=precision
    )


def chain_kernel(
    ndp, nmp,
    logits, ids_in, sp_hbm, kw_hbm, vw_hbm, q_hbm, k_hbm, v_hbm, c_hbm,
    att_out, tile_out, lg_out, w_out,
    p_v, kw_v, vw_v, q_v, k_v, v_v, c_v,
    mixed, ids_buf, sbuf, pair, gr, rbuf, ys, yr, zs, zr, wp, wbuf,
    lsem, gs, gv, fs, fv, js, jv, bs, bv, cs, cv, us, uv, ts, tv, ws, wv,
):
    n = ndp * nmp
    nz = nmp // 2
    width = kw_v.shape[1]
    rows = p_v.shape[1]
    nsrc = p_v.shape[0]
    ntask = logits.shape[0]
    tp = ntask * rows
    spn = nsrc * rows
    seq = q_v.shape[0]
    d = lax.axis_index("dp")
    m = lax.axis_index("mp")
    z = m // 2
    y = m % 2
    me = d * nmp + m
    other = z * 2 + (1 - y)

    def remote(src, dst, ss, rs, dd, mm_):
        return pltpu.make_async_remote_copy(
            src_ref=src, dst_ref=dst, send_sem=ss, recv_sem=rs,
            device_id=(dd, mm_), device_id_type=pl.DeviceIdType.MESH,
        )

    barrier = pltpu.get_barrier_semaphore()

    @pl.loop(1, n)
    def _(k):
        to = lax.rem(me + k, n)
        pl.semaphore_signal(
            barrier, inc=1, device_id=(to // nmp, lax.rem(to, nmp)),
            device_id_type=pl.DeviceIdType.MESH,
        )

    loads = [
        pltpu.make_async_copy(
            sp_hbm.at[:, pl.ds(pl.multiple_of(d * rows, rows), rows), :], p_v, lsem.at[0]
        )
    ]
    for i, (a, b) in enumerate(
        ((kw_hbm, kw_v), (vw_hbm, vw_v), (k_hbm, k_v), (q_hbm, q_v), (v_hbm, v_v), (c_hbm, c_v))
    ):
        loads.append(pltpu.make_async_copy(a, b, lsem.at[1 + i]))
    for c in loads:
        c.start()

    lg = logits[...]
    ex = jnp.exp(lg - jnp.max(lg, axis=1, keepdims=True))
    mix = ex / jnp.sum(ex, axis=1, keepdims=True)
    up = (
        lax.broadcasted_iota(jnp.int32, (tp, ntask), 0) // rows
        == lax.broadcasted_iota(jnp.int32, (tp, ntask), 1)
    )
    tall = mm(jnp.where(up, 1.0, 0.0), mix.astype(BF).astype(F32)).astype(BF)
    out = (
        lax.broadcasted_iota(jnp.int32, (nsrc, spn), 1) // rows
        == lax.broadcasted_iota(jnp.int32, (nsrc, spn), 0)
    )
    wide = mm(tall, jnp.where(out, 1.0, 0.0).astype(BF))
    same = (
        lax.broadcasted_iota(jnp.int32, (tp, spn), 0) % rows
        == lax.broadcasted_iota(jnp.int32, (tp, spn), 1) % rows
    )
    w_out[...] = jnp.where(same, wide, 0.0).astype(BF)
    ids_buf[d] = ids_in[...]

    loads[0].wait()
    mixed[m] = mm(w_out[...], p_v[...].reshape(spn, width)).astype(BF)

    pl.semaphore_wait(barrier, n - 1)

    idc = []
    for j in range(1, ndp):
        c = remote(ids_in, ids_buf.at[d], js.at[j], jv.at[j], lax.rem(d + j, ndp), m)
        c.start()
        idc.append(c)
    gat = []
    for j in range(1, nz):
        c = remote(
            mixed.at[m], mixed.at[m], gs.at[j], gv.at[j], d, lax.rem(z + j, nz) * 2 + y
        )
        c.start()
        gat.append(c)
    fwd = [remote(mixed.at[m], mixed.at[m], fs.at[0], fv.at[0], d, other)]
    fwd[0].start()
    for c in idc:
        c.wait()
    loads[1].wait()
    loads[2].wait()

    def part(slot):
        block = mixed[slot]
        at = pl.ds(pl.multiple_of(slot * width, width), width)
        return mm(block, kw_v[at, :]), mm(block, vw_v[at, :])

    pk, pv = part(m)
    for j in range(1, nz):
        slot = lax.rem(z + nz - j, nz) * 2 + y
        gat[j - 1].wait_recv()
        c = remote(mixed.at[slot], mixed.at[slot], fs.at[j], fv.at[j], d, other)
        c.start()
        fwd.append(c)
        a, b = part(slot)
        pk, pv = pk + a, pv + b
    for j in range(nz):
        slot = lax.rem(z + nz - j, nz) * 2 + (1 - y)
        fwd[j].wait_recv()
        a, b = part(slot)
        pk, pv = pk + a, pv + b

    ids_all = ids_buf[...].reshape(n, tp).astype(BF)
    rep = (
        lax.broadcasted_iota(jnp.int32, (n * rows, n), 0) // rows
        == lax.broadcasted_iota(jnp.int32, (n * rows, n), 1)
    )
    ids_x = mm(jnp.where(rep, 1.0, 0.0).astype(BF), ids_all)
    lane = lax.broadcasted_iota(jnp.int32, (n * rows, tp), 1)
    row = lax.broadcasted_iota(jnp.int32, (n * rows, tp), 0)
    sel = jnp.where(
        (ids_x == (lane // rows).astype(F32)) & (lane % rows == row % rows), 1.0, 0.0
    ).astype(BF)
    sbuf[:, 0] = mm(sel, pk.astype(BF)).astype(BF).reshape(n, rows, width)
    sbuf[:, 1] = mm(sel, pv.astype(BF)).astype(BF).reshape(n, rows, width)

    my_rows = pl.ds(pl.multiple_of(d * rows, rows), rows)
    my_cols = pl.ds(pl.multiple_of(m * width, width), width)

    def b_copy(k):
        dd, gg = lax.rem(k, ndp), k // ndp
        td, tm = lax.rem(d + ndp - dd, ndp), lax.rem(m + nmp - gg, nmp)
        return remote(
            sbuf.at[td * nmp + tm], pair.at[:, my_rows, my_cols], bs.at[k], bv.at[k], td, tm
        )

    own_b = pltpu.make_async_copy(sbuf.at[me], pair.at[:, my_rows, my_cols], lsem.at[7])
    own_b.start()

    @pl.loop(1, n)
    def _(k):
        b_copy(k).start()

    for c in loads[3:]:
        c.wait()
    own_b.wait()

    def c_copy(k):
        dd, gg = lax.rem(k, ndp), k // ndp
        td, tm = lax.rem(d + dd, ndp), lax.rem(m + gg, nmp)
        return remote(
            gr.at[
                :,
                pl.ds(pl.multiple_of(td * rows, rows), rows),
                pl.ds(pl.multiple_of(tm * width, width), width),
            ],
            rbuf.at[me], cs.at[k], cv.at[k], td, tm,
        )

    scale = DH ** (-0.5)
    seen = lax.broadcasted_iota(jnp.int32, (seq, seq), 1) <= lax.broadcasted_iota(
        jnp.int32, (seq, seq), 0
    )

    def group(g, wait_from):
        @pl.loop(wait_from, ndp)
        def _(dd):
            b_copy(g * ndp + dd).wait_recv()

        base = lax.rem(m + g, nmp) * width
        for h in range(width // DH):
            at = pl.ds(pl.multiple_of(base + h * DH, DH), DH)
            q, c, kk, vv = q_v[:, at], c_v[:, at], k_v[:, at], v_v[:, at]
            kp, vp = pair[0, :, at], pair[1, :, at]
            s1 = mm(q, kp, 1, 1) * scale
            s2 = jnp.where(seen, mm(q, kk, 1, 1) * scale, mask_fill)
            top = jnp.maximum(
                jnp.max(s1, axis=1, keepdims=True), jnp.max(s2, axis=1, keepdims=True)
            )
            e1, e2 = jnp.exp(s1 - top), jnp.exp(s2 - top)
            inv = 1.0 / (
                jnp.sum(e1, axis=1, keepdims=True) + jnp.sum(e2, axis=1, keepdims=True)
            )
            a1, a2 = e1 * inv, e2 * inv
            b1 = a1.astype(BF)
            att_out[:, at] = (mm(b1, vp) + mm(a2.astype(BF), vv)).astype(BF)
            g1, g2 = mm(c, vp, 1, 1), mm(c, vv, 1, 1)
            inner = jnp.sum(a1 * g1, axis=1, keepdims=True) + jnp.sum(
                a2 * g2, axis=1, keepdims=True
            )
            gs1 = (a1 * (g1 - inner)).astype(BF)
            gr[0, :, at] = (mm(gs1, q, 0, 0) * scale).astype(BF)
            gr[1, :, at] = mm(b1, c, 0, 0).astype(BF)

    group(0, 1)
    own_c = pltpu.make_async_copy(gr.at[:, my_rows, my_cols], rbuf.at[me], lsem.at[8])
    own_c.start()

    @pl.loop(1, ndp)
    def _(dd):
        c_copy(dd).start()

    @pl.loop(1, nmp)
    def _(g):
        group(g, 0)

        @pl.loop(0, ndp)
        def _(dd):
            c_copy(g * ndp + dd).start()

    own_c.wait()

    @pl.loop(1, n)
    def _(k):
        c_copy(k).wait_recv()

    tk = mm(sel, rbuf[:, 0].reshape(n * rows, width), 0, 0).astype(BF)
    tv_ = mm(sel, rbuf[:, 1].reshape(n * rows, width), 0, 0).astype(BF)

    def term(slot):
        at = pl.ds(pl.multiple_of(slot * width, width), width)
        return mm(tk, kw_v[at, :], 1, 1) + mm(tv_, vw_v[at, :], 1, 1)

    yc, zc = [None] * nz, [None] * nz
    order = list(range(1, nz)) + [0]
    for j in order:
        ys[j] = term(lax.rem(z + j, nz) * 2 + (1 - y)).astype(BF)
        yc[j] = remote(ys.at[j], yr.at[j], us.at[j], uv.at[j], d, other)
        yc[j].start()
    for j in order:
        to = lax.rem(z + j, nz) * 2 + y
        mine = term(to)
        yc[j].wait_recv()
        mine = mine + yr[j].astype(F32)
        if j:
            zs[j] = mine.astype(BF)
            zc[j] = remote(zs.at[j], zr.at[j], ts.at[j], tv.at[j], d, to)
            zc[j].start()
    for j in range(1, nz):
        zc[j].wait_recv()
        mine = mine + zr[j].astype(F32)
    tile = mine.astype(BF)
    tile_out[...] = tile

    prod = mm(p_v[...].reshape(spn, width), tile, 1, 1)
    same_t = (
        lax.broadcasted_iota(jnp.int32, (spn, tp), 0) % rows
        == lax.broadcasted_iota(jnp.int32, (spn, tp), 1) % rows
    )
    prod = jnp.sum(jnp.where(same_t, prod, 0.0).reshape(nsrc, rows, tp), axis=1)
    fold = (
        lax.broadcasted_iota(jnp.int32, (ntask, tp), 1) // rows
        == lax.broadcasted_iota(jnp.int32, (ntask, tp), 0)
    )
    part_w = mm(jnp.where(fold, 1.0, 0.0), prod, 1, 1, lax.Precision.HIGHEST)
    wp[...] = part_w
    wbuf[me] = part_w

    def w_copy(k):
        to = lax.rem(me + k, n)
        return remote(wp, wbuf.at[me], ws.at[k], wv.at[k], to // nmp, lax.rem(to, nmp))

    @pl.loop(1, n)
    def _(k):
        w_copy(k).start()

    for c in idc + gat + fwd:
        pass
    for c in gat + fwd + yc + zc[1:]:
        c.wait_send()

    @pl.loop(1, n)
    def _(k):
        b_copy(k).wait_send()
        c_copy(k).wait_send()

    @pl.loop(1, n)
    def _(k):
        w_copy(k).wait()

    wg = jnp.sum(wbuf[...], axis=0)
    lg_out[...] = mix * (wg - jnp.sum(mix * wg, axis=1, keepdims=True))


def source_kernel(w_ref, tile_ref, out_ref):
    got = mm(w_ref[...], tile_ref[...], 0, 0)
    out_ref[...] = got.reshape(out_ref.shape)


def per_device(ndp, nmp, *args):
    source_prompts, task_logits, task_ids, key_weight, value_weight = args[:5]
    queries, keys, values, cotangent = args[5:]
    nsrc, ptok, width = source_prompts.shape
    ntask = task_logits.shape[0]
    ge = task_ids.shape[0]
    rows = ptok // ndp
    if width % DH or nmp % 2 or ge != nmp or ptok % ndp or rows % 16 or ntask * rows != 128:
        return on_device(*args)
    n, nz = ndp * nmp, nmp // 2
    tp, spn = ntask * rows, nsrc * rows
    seq, full = queries.shape[1:]
    ids_tile = jnp.broadcast_to(task_ids.astype(F32)[:, None], (ge, tp))
    vmem = pl.BlockSpec(memory_space=pltpu.VMEM)
    hbm = pl.BlockSpec(memory_space=pl.ANY)
    dma = pltpu.SemaphoreType.DMA
    attended, tile, logits_grad, w_big = pl.pallas_call(
        functools.partial(chain_kernel, ndp, nmp),
        out_shape=(
            jax.ShapeDtypeStruct((seq, full), BF),
            jax.ShapeDtypeStruct((tp, width), BF),
            jax.ShapeDtypeStruct((ntask, nsrc), F32),
            jax.ShapeDtypeStruct((tp, spn), BF),
        ),
        in_specs=[vmem, vmem] + [hbm] * 7,
        out_specs=(vmem,) * 4,
        scratch_shapes=[
            pltpu.VMEM((nsrc, rows, width), BF),
            pltpu.VMEM((full, width), BF),
            pltpu.VMEM((full, width), BF),
            pltpu.VMEM((seq, full), BF),
            pltpu.VMEM((seq, full), BF),
            pltpu.VMEM((seq, full), BF),
            pltpu.VMEM((seq, full), BF),
            pltpu.VMEM((nmp, tp, width), BF),
            pltpu.VMEM((ndp, ge, tp), F32),
            pltpu.VMEM((n, 2, rows, width), BF),
            pltpu.VMEM((2, ptok, full), BF),
            pltpu.VMEM((2, ptok, full), BF),
            pltpu.VMEM((n, 2, rows, width), BF),
            pltpu.VMEM((nz, tp, width), BF),
            pltpu.VMEM((nz, tp, width), BF),
            pltpu.VMEM((nz, tp, width), BF),
            pltpu.VMEM((nz, tp, width), BF),
            pltpu.VMEM((ntask, nsrc), F32),
            pltpu.VMEM((n, ntask, nsrc), F32),
            dma((9,)),
            dma((nz,)), dma((nz,)), dma((nz,)), dma((nz,)),
            dma((ndp,)), dma((ndp,)),
            dma((n,)), dma((n,)), dma((n,)), dma((n,)),
            dma((nz,)), dma((nz,)), dma((nz,)), dma((nz,)),
            dma((n,)), dma((n,)),
        ],
        compiler_params=pltpu.CompilerParams(
            collective_id=0, has_side_effects=True, vmem_limit_bytes=60 * 2**20
        ),
        name="chain",
    )(
        task_logits, ids_tile, source_prompts, key_weight, value_weight,
        queries.reshape(seq, full), keys.reshape(seq, full),
        values.reshape(seq, full), cotangent.reshape(seq, full),
    )
    steps = 8
    source_grad = pl.pallas_call(
        source_kernel,
        grid=(steps,),
        out_shape=jax.ShapeDtypeStruct((nsrc, rows, width), F32),
        in_specs=[
            pl.BlockSpec((tp, spn // steps), lambda i: (0, i)),
            pl.BlockSpec((tp, width), lambda i: (0, 0)),
        ],
        out_specs=pl.BlockSpec((nsrc // steps, rows, width), lambda i: (i, 0, 0)),
        name="source_grad",
    )(w_big, tile)
    return (attended.reshape(queries.shape), source_grad, logits_grad)


def solution(mesh):
    placed = (
        P(None, None, "mp"),
        P(),
        P("dp"),
        P(None, "mp"),
        P(None, "mp"),
        P(("dp", "mp"), None, None),
        P(("dp", "mp"), None, None),
        P(("dp", "mp"), None, None),
        P(("dp", "mp"), None, None),
    )
    return jax.shard_map(
        functools.partial(per_device, mesh.shape["dp"], mesh.shape["mp"]),
        mesh=mesh,
        in_specs=placed,
        out_specs=(P(("dp", "mp"), None, None), P(None, "dp", "mp"), P()),
        check_vma=False,
    )
```

```python
import functools

import jax
import jax.numpy as jnp
from jax import lax
from jax.experimental import pallas as pl
from jax.experimental.pallas import tpu as pltpu
from jax.sharding import PartitionSpec as P

D = 4096
HEADS = 32
DH = 128
NSRC = 128
NTASK = 8
PTOK = 64
SEQ = 128
E_DEV = 1


mask_fill = -1e30


def example_block(prompt_pair, queries, keys, values, cotangent):
    examples = queries.shape[0]
    score_scale = DH ** (-0.5)
    key_all = jnp.concatenate([prompt_pair[:, :, 0, :], keys], axis=1)
    value_all = jnp.concatenate([prompt_pair[:, :, 1, :], values], axis=1)
    query_heads = queries.reshape(examples, SEQ, HEADS, DH)
    key_heads = key_all.reshape(examples, PTOK + SEQ, HEADS, DH)
    value_heads = value_all.reshape(examples, PTOK + SEQ, HEADS, DH)
    cot_heads = cotangent.reshape(examples, SEQ, HEADS, DH)
    scores = (
        jnp.einsum("eihd,ejhd->ehij", query_heads, key_heads, preferred_element_type=jnp.float32)
        * score_scale
    )
    column = jnp.arange(PTOK + SEQ)[None, :]
    position = jnp.arange(SEQ)[:, None]
    visible = (column < PTOK) | (column - PTOK <= position)
    scores = jnp.where(visible[None, None], scores, mask_fill)
    top_score = jnp.max(scores, axis=3, keepdims=True)
    exponent = jnp.exp(scores - top_score)
    attention = exponent / jnp.sum(exponent, axis=3, keepdims=True)
    attention_rounded = attention.astype(jnp.bfloat16)
    attended = jnp.einsum(
        "ehij,ejhd->eihd", attention_rounded, value_heads, preferred_element_type=jnp.float32
    )
    attended = attended.astype(jnp.bfloat16).reshape(examples, SEQ, D)
    grad_attention = jnp.einsum(
        "eihd,ejhd->ehij", cot_heads, value_heads, preferred_element_type=jnp.float32
    )
    inner_sum = jnp.sum(attention * grad_attention, axis=3, keepdims=True)
    grad_scores = (attention * (grad_attention - inner_sum)).astype(jnp.bfloat16)
    key_grads = jnp.einsum(
        "ehij,eihd->ejhd",
        grad_scores[:, :, :, :PTOK],
        query_heads,
        preferred_element_type=jnp.float32,
    )
    key_grads = (key_grads * score_scale).astype(jnp.bfloat16).reshape(examples, PTOK, D)
    value_grads = jnp.einsum(
        "ehij,eihd->ejhd",
        attention_rounded[:, :, :, :PTOK],
        cot_heads,
        preferred_element_type=jnp.float32,
    )
    value_grads = value_grads.astype(jnp.bfloat16).reshape(examples, PTOK, D)
    return (attended, jnp.stack([key_grads, value_grads], axis=2))


def tile_products(tile_grad, source_prompts, mix_weights, col_width):
    rows_here = tile_grad.shape[1]
    own_prompts = lax.dynamic_slice_in_dim(
        source_prompts, lax.axis_index("dp") * rows_here, rows_here, 1
    )
    tile_flat = tile_grad.reshape(NTASK, rows_here * col_width)
    source_grad = jnp.dot(mix_weights.T, tile_flat, precision=lax.Precision.HIGHEST)
    source_grad = source_grad.reshape(NSRC, rows_here, col_width)
    weight_part = jnp.dot(
        tile_flat,
        own_prompts.reshape(NSRC, rows_here * col_width).astype(jnp.float32).T,
        precision=lax.Precision.HIGHEST,
    )
    return (source_grad, weight_part)


def on_device(
    source_prompts,
    task_logits,
    task_ids,
    key_weight,
    value_weight,
    queries,
    keys,
    values,
    cotangent,
):
    col_width = key_weight.shape[1]
    group_examples = task_ids.shape[0]
    mix_weights = jax.nn.softmax(task_logits, axis=1)
    mix_rounded = mix_weights.astype(jnp.bfloat16)
    mixture = jnp.dot(
        mix_rounded,
        source_prompts.reshape(NSRC, PTOK * col_width),
        preferred_element_type=jnp.float32,
    )
    mixture = mixture.astype(jnp.bfloat16).reshape(NTASK, PTOK, col_width)
    pair_weight = jnp.concatenate([key_weight, value_weight], axis=1)
    portion = lax.all_gather(mixture, "mp", axis=2, tiled=True)
    portion_rows = portion.reshape(NTASK * PTOK, portion.shape[2])
    projected = jnp.dot(portion_rows, pair_weight, preferred_element_type=jnp.float32)
    projected = projected.astype(jnp.bfloat16).reshape(NTASK, PTOK, 2, col_width)
    task_range = jnp.arange(NTASK, dtype=jnp.int32)
    selector_all = (task_ids[:, None] == task_range[None, :]).astype(jnp.bfloat16)
    table_full = lax.all_gather(projected, "mp", axis=3, tiled=True)
    own_offset = lax.axis_index("mp") * E_DEV
    own_selector = lax.dynamic_slice_in_dim(selector_all, own_offset, E_DEV, 0)
    chosen = jnp.dot(
        own_selector, table_full.reshape(NTASK, PTOK * 2 * D), preferred_element_type=jnp.float32
    )
    prompt_pair = chosen.astype(jnp.bfloat16).reshape(E_DEV, PTOK, 2, D)
    attended, outgoing_grads = example_block(prompt_pair, queries, keys, values, cotangent)
    incoming = lax.all_to_all(outgoing_grads, "mp", split_axis=3, concat_axis=0, tiled=True)
    group_grads = jnp.dot(
        selector_all.T,
        incoming.reshape(group_examples, PTOK * 2 * col_width),
        preferred_element_type=jnp.float32,
    )
    pair_weight_t = pair_weight.astype(jnp.float32).T
    task_rows = lax.psum_scatter(
        group_grads.reshape(NTASK, PTOK, 2 * col_width), "dp", scatter_dimension=1, tiled=True
    )
    rows_here = task_rows.shape[1]
    row_terms = jnp.dot(
        task_rows.reshape(NTASK * rows_here, 2 * col_width),
        pair_weight_t,
        precision=lax.Precision.HIGHEST,
    ).reshape(NTASK, rows_here, D)
    tile_grad = lax.psum_scatter(row_terms, "mp", scatter_dimension=2, tiled=True)
    source_grad, weight_part = tile_products(tile_grad, source_prompts, mix_weights, col_width)
    weight_grad = lax.psum(weight_part, ("dp", "mp"))
    logits_grad = mix_weights * (
        weight_grad - jnp.sum(mix_weights * weight_grad, axis=1, keepdims=True)
    )
    return (attended, source_grad, logits_grad)


BF = jnp.bfloat16
F32 = jnp.float32


def mm(a, b, ca=1, cb=0, precision=None):
    return lax.dot_general(
        a, b, (((ca,), (cb,)), ((), ())), preferred_element_type=F32, precision=precision
    )


def chain_kernel(
    ndp, nmp,
    logits, ids_in, sp_hbm, kw_hbm, vw_hbm, q_hbm, k_hbm, v_hbm, c_hbm,
    att_out, tile_out, lg_out, w_out,
    p_v, kw_v, vw_v, q_v, k_v, v_v, c_v,
    mixed, ids_own, ids_buf, sbuf, pair, gr, rbuf, ys, yr, zs, zr, wp, wbuf,
    lsem, gs, gv, fs, fv, js, jv, bs, bv, cs, cv, us, uv, ts, tv, ws, wv,
):
    n = ndp * nmp
    nz = nmp // 2
    width = kw_v.shape[1]
    rows = p_v.shape[1]
    nsrc = p_v.shape[0]
    ntask = logits.shape[0]
    tp = ntask * rows
    spn = nsrc * rows
    seq = q_v.shape[0]
    d = lax.axis_index("dp")
    m = lax.axis_index("mp")
    z = m // 2
    y = m % 2
    me = d * nmp + m
    other = z * 2 + (1 - y)

    shift = rows.bit_length() - 1

    def iota(shape, axis):
        return lax.broadcasted_iota(jnp.int32, shape, axis)

    def outer(a):
        return lax.shift_right_logical(a, jnp.int32(shift))

    def same_row(shape):
        return ((iota(shape, 0) ^ iota(shape, 1)) & (rows - 1)) == 0

    def remote(src, dst, ss, rs, dd, mm_):
        return pltpu.make_async_remote_copy(
            src_ref=src, dst_ref=dst, send_sem=ss, recv_sem=rs,
            device_id=(dd, mm_), device_id_type=pl.DeviceIdType.MESH,
        )

    barrier = pltpu.get_barrier_semaphore()

    @pl.loop(1, n)
    def _(k):
        to = lax.rem(me + k, n)
        pl.semaphore_signal(
            barrier, inc=1, device_id=(to // nmp, lax.rem(to, nmp)),
            device_id_type=pl.DeviceIdType.MESH,
        )

    loads = [
        pltpu.make_async_copy(
            sp_hbm.at[:, pl.ds(pl.multiple_of(d * rows, rows), rows), :], p_v, lsem.at[0]
        )
    ]
    for i, (a, b) in enumerate(
        ((kw_hbm, kw_v), (vw_hbm, vw_v), (k_hbm, k_v), (q_hbm, q_v), (v_hbm, v_v), (c_hbm, c_v))
    ):
        loads.append(pltpu.make_async_copy(a, b, lsem.at[1 + i]))
    loads[0].start()

    lg = logits[...]
    ex = jnp.exp(lg - jnp.max(lg, axis=1, keepdims=True))
    mix = ex / jnp.sum(ex, axis=1, keepdims=True)
    up = (
        outer(iota((tp, ntask), 0)) == iota((tp, ntask), 1)
    )
    tall = mm(jnp.where(up, 1.0, 0.0), mix.astype(BF).astype(F32)).astype(BF)
    out = (
        outer(iota((nsrc, spn), 1)) == iota((nsrc, spn), 0)
    )
    wide = mm(tall, jnp.where(out, 1.0, 0.0).astype(BF))
    w_out[...] = jnp.where(same_row((tp, spn)), wide, 0.0).astype(BF)
    for j in range(ids_in.shape[0]):
        line = jnp.full((1, tp), ids_in[j], jnp.int32).astype(F32)
        ids_own[pl.ds(j, 1), :] = line
        ids_buf[d, pl.ds(j, 1), :] = line

    loads[0].wait()
    for c in loads[1:]:
        c.start()
    mixed[m] = mm(w_out[...], p_v[...].reshape(spn, width)).astype(BF)

    pl.semaphore_wait(barrier, n - 1)

    idc = []
    for j in range(1, ndp):
        c = remote(ids_own, ids_buf.at[d], js.at[j], jv.at[j], lax.rem(d + j, ndp), m)
        c.start()
        idc.append(c)
    gat = []
    for j in range(1, nz):
        c = remote(
            mixed.at[m], mixed.at[m], gs.at[j], gv.at[j], d, lax.rem(z + j, nz) * 2 + y
        )
        c.start()
        gat.append(c)
    fwd = [remote(mixed.at[m], mixed.at[m], fs.at[0], fv.at[0], d, other)]
    fwd[0].start()
    for c in idc:
        c.wait()
    loads[1].wait()
    loads[2].wait()

    def part(slot):
        block = mixed[slot]
        at = pl.ds(pl.multiple_of(slot * width, width), width)
        return mm(block, kw_v[at, :]), mm(block, vw_v[at, :])

    pk, pv = part(m)
    for j in range(1, nz):
        slot = lax.rem(z + nz - j, nz) * 2 + y
        gat[j - 1].wait_recv()
        c = remote(mixed.at[slot], mixed.at[slot], fs.at[j], fv.at[j], d, other)
        c.start()
        fwd.append(c)
        a, b = part(slot)
        pk, pv = pk + a, pv + b
    for j in range(nz):
        slot = lax.rem(z + nz - j, nz) * 2 + (1 - y)
        fwd[j].wait_recv()
        a, b = part(slot)
        pk, pv = pk + a, pv + b

    ids_all = ids_buf[...].reshape(n, tp).astype(BF)
    rep = (
        outer(iota((n * rows, n), 0)) == iota((n * rows, n), 1)
    )
    ids_x = mm(jnp.where(rep, 1.0, 0.0).astype(BF), ids_all)
    sel = jnp.where(
        (ids_x == outer(iota((n * rows, tp), 1)).astype(F32)) & same_row((n * rows, tp)), 1.0, 0.0
    ).astype(BF)
    sbuf[:, 0] = mm(sel, pk.astype(BF)).astype(BF).reshape(n, rows, width)
    sbuf[:, 1] = mm(sel, pv.astype(BF)).astype(BF).reshape(n, rows, width)

    my_rows = pl.ds(pl.multiple_of(d * rows, rows), rows)
    my_cols = pl.ds(pl.multiple_of(m * width, width), width)

    def b_copy(k):
        dd, gg = lax.rem(k, ndp), k // ndp
        td, tm = lax.rem(d + ndp - dd, ndp), lax.rem(m + nmp - gg, nmp)
        return remote(
            sbuf.at[td * nmp + tm], pair.at[:, my_rows, my_cols], bs.at[k], bv.at[k], td, tm
        )

    own_b = pltpu.make_async_copy(sbuf.at[me], pair.at[:, my_rows, my_cols], lsem.at[7])
    own_b.start()

    @pl.loop(1, n)
    def _(k):
        b_copy(k).start()

    for c in loads[3:]:
        c.wait()
    own_b.wait()

    def c_copy(k):
        dd, gg = lax.rem(k, ndp), k // ndp
        td, tm = lax.rem(d + dd, ndp), lax.rem(m + gg, nmp)
        return remote(
            gr.at[
                :,
                pl.ds(pl.multiple_of(td * rows, rows), rows),
                pl.ds(pl.multiple_of(tm * width, width), width),
            ],
            rbuf.at[me], cs.at[k], cv.at[k], td, tm,
        )

    scale = DH ** (-0.5)
    to_exp2 = scale * 1.4426950408889634
    ptok = pair.shape[1]
    seen = iota((seq, seq), 0) <= iota((seq, seq), 1)

    def group(g, wait_from):
        @pl.loop(wait_from, ndp)
        def _(dd):
            b_copy(g * ndp + dd).wait_recv()

        base = lax.rem(m + g, nmp) * width
        ats, st, gt, va = [], [], [], []
        for h in range(width // DH):
            at = pl.ds(pl.multiple_of(base + h * DH, DH), DH)
            ats.append(at)
            ka = jnp.concatenate([pair[0, :, at], k_v[:, at]], axis=0)
            va.append(jnp.concatenate([pair[1, :, at], v_v[:, at]], axis=0))
            st.append(mm(ka, q_v[:, at], 1, 1))
            gt.append(mm(va[h], c_v[:, at], 1, 1))
        for h in range(width // DH):
            at = ats[h]
            s = st[h] * to_exp2
            s = jnp.concatenate([s[:ptok], jnp.where(seen, s[ptok:], mask_fill)], axis=0)
            e = jnp.exp2(s - jnp.max(s, axis=0, keepdims=True))
            a = e * (1.0 / jnp.sum(e, axis=0, keepdims=True))
            ab = a.astype(BF)
            inner = jnp.sum(a * gt[h], axis=0, keepdims=True)
            gs1 = (a[:ptok] * (gt[h][:ptok] - inner)).astype(BF)
            gr[0, :, at] = (mm(gs1, q_v[:, at]) * scale).astype(BF)
            gr[1, :, at] = mm(ab[:ptok], c_v[:, at]).astype(BF)
            att_out[:, at] = mm(ab, va[h], 0, 0).astype(BF)

    group(0, 1)
    own_c = pltpu.make_async_copy(gr.at[:, my_rows, my_cols], rbuf.at[me], lsem.at[8])
    own_c.start()

    @pl.loop(1, ndp)
    def _(dd):
        c_copy(dd).start()

    @pl.loop(1, nmp)
    def _(g):
        group(g, 0)

        @pl.loop(0, ndp)
        def _(dd):
            c_copy(g * ndp + dd).start()

    own_c.wait()

    @pl.loop(1, n)
    def _(k):
        c_copy(k).wait_recv()

    tk = mm(sel, rbuf[:, 0].reshape(n * rows, width), 0, 0).astype(BF)
    tv_ = mm(sel, rbuf[:, 1].reshape(n * rows, width), 0, 0).astype(BF)

    def term(slot):
        at = pl.ds(pl.multiple_of(slot * width, width), width)
        return mm(tk, kw_v[at, :], 1, 1) + mm(tv_, vw_v[at, :], 1, 1)

    yc, zc = [None] * nz, [None] * nz
    order = list(range(1, nz)) + [0]
    for j in order:
        ys[j] = term(lax.rem(z + j, nz) * 2 + (1 - y)).astype(BF)
        yc[j] = remote(ys.at[j], yr.at[j], us.at[j], uv.at[j], d, other)
        yc[j].start()
    for j in order:
        to = lax.rem(z + j, nz) * 2 + y
        mine = term(to)
        yc[j].wait_recv()
        mine = mine + yr[j].astype(F32)
        if j:
            zs[j] = mine.astype(BF)
            zc[j] = remote(zs.at[j], zr.at[j], ts.at[j], tv.at[j], d, to)
            zc[j].start()
    for j in range(1, nz):
        zc[j].wait_recv()
        mine = mine + zr[j].astype(F32)
    tile = mine.astype(BF)
    tile_out[...] = tile

    prod = mm(p_v[...].reshape(spn, width), tile, 1, 1)
    prod = jnp.sum(jnp.where(same_row((spn, tp)), prod, 0.0).reshape(nsrc, rows, tp), axis=1)
    fold = (
        outer(iota((ntask, tp), 1)) == iota((ntask, tp), 0)
    )
    part_w = mm(jnp.where(fold, 1.0, 0.0), prod, 1, 1, lax.Precision.HIGHEST)
    wp[...] = part_w
    wbuf[me] = part_w

    def w_copy(k):
        to = lax.rem(me + k, n)
        return remote(wp, wbuf.at[me], ws.at[k], wv.at[k], to // nmp, lax.rem(to, nmp))

    @pl.loop(1, n)
    def _(k):
        w_copy(k).start()

    for c in gat + fwd + yc + zc[1:]:
        c.wait_send()

    @pl.loop(1, n)
    def _(k):
        b_copy(k).wait_send()
        c_copy(k).wait_send()

    @pl.loop(1, n)
    def _(k):
        w_copy(k).wait()

    wg = jnp.sum(wbuf[...], axis=0)
    lg_out[...] = mix * (wg - jnp.sum(mix * wg, axis=1, keepdims=True))


def source_kernel(w_ref, tile_ref, out_ref):
    got = mm(w_ref[...], tile_ref[...], 0, 0)
    out_ref[...] = got.reshape(out_ref.shape)


def per_device(ndp, nmp, *args):
    source_prompts, task_logits, task_ids, key_weight, value_weight = args[:5]
    queries, keys, values, cotangent = args[5:]
    nsrc, ptok, width = source_prompts.shape
    ntask = task_logits.shape[0]
    ge = task_ids.shape[0]
    rows = ptok // ndp
    if width % DH or nmp % 2 or ge != nmp or ptok % ndp or rows % 16 or rows & (rows - 1) or ntask * rows != 128:
        return on_device(*args)
    n, nz = ndp * nmp, nmp // 2
    tp, spn = ntask * rows, nsrc * rows
    seq, full = queries.shape[1:]
    vmem = pl.BlockSpec(memory_space=pltpu.VMEM)
    hbm = pl.BlockSpec(memory_space=pl.ANY)
    dma = pltpu.SemaphoreType.DMA
    attended, tile, logits_grad, w_big = pl.pallas_call(
        functools.partial(chain_kernel, ndp, nmp),
        out_shape=(
            jax.ShapeDtypeStruct((seq, full), BF),
            jax.ShapeDtypeStruct((tp, width), BF),
            jax.ShapeDtypeStruct((ntask, nsrc), F32),
            jax.ShapeDtypeStruct((tp, spn), BF),
        ),
        in_specs=[vmem, pl.BlockSpec(memory_space=pltpu.SMEM)] + [hbm] * 7,
        out_specs=(vmem,) * 4,
        scratch_shapes=[
            pltpu.VMEM((nsrc, rows, width), BF),
            pltpu.VMEM((full, width), BF),
            pltpu.VMEM((full, width), BF),
            pltpu.VMEM((seq, full), BF),
            pltpu.VMEM((seq, full), BF),
            pltpu.VMEM((seq, full), BF),
            pltpu.VMEM((seq, full), BF),
            pltpu.VMEM((nmp, tp, width), BF),
            pltpu.VMEM((ge, tp), F32),
            pltpu.VMEM((ndp, ge, tp), F32),
            pltpu.VMEM((n, 2, rows, width), BF),
            pltpu.VMEM((2, ptok, full), BF),
            pltpu.VMEM((2, ptok, full), BF),
            pltpu.VMEM((n, 2, rows, width), BF),
            pltpu.VMEM((nz, tp, width), BF),
            pltpu.VMEM((nz, tp, width), BF),
            pltpu.VMEM((nz, tp, width), BF),
            pltpu.VMEM((nz, tp, width), BF),
            pltpu.VMEM((ntask, nsrc), F32),
            pltpu.VMEM((n, ntask, nsrc), F32),
            dma((9,)),
            dma((nz,)), dma((nz,)), dma((nz,)), dma((nz,)),
            dma((ndp,)), dma((ndp,)),
            dma((n,)), dma((n,)), dma((n,)), dma((n,)),
            dma((nz,)), dma((nz,)), dma((nz,)), dma((nz,)),
            dma((n,)), dma((n,)),
        ],
        compiler_params=pltpu.CompilerParams(
            collective_id=0, has_side_effects=True, vmem_limit_bytes=60 * 2**20
        ),
        name="chain",
    )(
        task_logits, task_ids, source_prompts, key_weight, value_weight,
        queries.reshape(seq, full), keys.reshape(seq, full),
        values.reshape(seq, full), cotangent.reshape(seq, full),
    )
    steps = 4
    source_grad = pl.pallas_call(
        source_kernel,
        grid=(steps,),
        out_shape=jax.ShapeDtypeStruct((nsrc, rows, width), F32),
        in_specs=[
            pl.BlockSpec((tp, spn // steps), lambda i: (0, i)),
            pl.BlockSpec((tp, width), lambda i: (0, 0)),
        ],
        out_specs=pl.BlockSpec((nsrc // steps, rows, width), lambda i: (i, 0, 0)),
        name="source_grad",
    )(w_big, tile)
    return (attended.reshape(queries.shape), source_grad, logits_grad)


def solution(mesh):
    placed = (
        P(None, None, "mp"),
        P(),
        P("dp"),
        P(None, "mp"),
        P(None, "mp"),
        P(("dp", "mp"), None, None),
        P(("dp", "mp"), None, None),
        P(("dp", "mp"), None, None),
        P(("dp", "mp"), None, None),
    )
    return jax.shard_map(
        functools.partial(per_device, mesh.shape["dp"], mesh.shape["mp"]),
        mesh=mesh,
        in_specs=placed,
        out_specs=(P(("dp", "mp"), None, None), P(None, "dp", "mp"), P()),
        check_vma=False,
    )
```

```python
import functools

import jax
import jax.numpy as jnp
from jax import lax
from jax.experimental import pallas as pl
from jax.experimental.pallas import tpu as pltpu
from jax.sharding import PartitionSpec as P

D = 4096
HEADS = 32
DH = 128
NSRC = 128
NTASK = 8
PTOK = 64
SEQ = 128
E_DEV = 1


mask_fill = -1e30


def example_block(prompt_pair, queries, keys, values, cotangent):
    examples = queries.shape[0]
    score_scale = DH ** (-0.5)
    key_all = jnp.concatenate([prompt_pair[:, :, 0, :], keys], axis=1)
    value_all = jnp.concatenate([prompt_pair[:, :, 1, :], values], axis=1)
    query_heads = queries.reshape(examples, SEQ, HEADS, DH)
    key_heads = key_all.reshape(examples, PTOK + SEQ, HEADS, DH)
    value_heads = value_all.reshape(examples, PTOK + SEQ, HEADS, DH)
    cot_heads = cotangent.reshape(examples, SEQ, HEADS, DH)
    scores = (
        jnp.einsum("eihd,ejhd->ehij", query_heads, key_heads, preferred_element_type=jnp.float32)
        * score_scale
    )
    column = jnp.arange(PTOK + SEQ)[None, :]
    position = jnp.arange(SEQ)[:, None]
    visible = (column < PTOK) | (column - PTOK <= position)
    scores = jnp.where(visible[None, None], scores, mask_fill)
    top_score = jnp.max(scores, axis=3, keepdims=True)
    exponent = jnp.exp(scores - top_score)
    attention = exponent / jnp.sum(exponent, axis=3, keepdims=True)
    attention_rounded = attention.astype(jnp.bfloat16)
    attended = jnp.einsum(
        "ehij,ejhd->eihd", attention_rounded, value_heads, preferred_element_type=jnp.float32
    )
    attended = attended.astype(jnp.bfloat16).reshape(examples, SEQ, D)
    grad_attention = jnp.einsum(
        "eihd,ejhd->ehij", cot_heads, value_heads, preferred_element_type=jnp.float32
    )
    inner_sum = jnp.sum(attention * grad_attention, axis=3, keepdims=True)
    grad_scores = (attention * (grad_attention - inner_sum)).astype(jnp.bfloat16)
    key_grads = jnp.einsum(
        "ehij,eihd->ejhd",
        grad_scores[:, :, :, :PTOK],
        query_heads,
        preferred_element_type=jnp.float32,
    )
    key_grads = (key_grads * score_scale).astype(jnp.bfloat16).reshape(examples, PTOK, D)
    value_grads = jnp.einsum(
        "ehij,eihd->ejhd",
        attention_rounded[:, :, :, :PTOK],
        cot_heads,
        preferred_element_type=jnp.float32,
    )
    value_grads = value_grads.astype(jnp.bfloat16).reshape(examples, PTOK, D)
    return (attended, jnp.stack([key_grads, value_grads], axis=2))


def tile_products(tile_grad, source_prompts, mix_weights, col_width):
    rows_here = tile_grad.shape[1]
    own_prompts = lax.dynamic_slice_in_dim(
        source_prompts, lax.axis_index("dp") * rows_here, rows_here, 1
    )
    tile_flat = tile_grad.reshape(NTASK, rows_here * col_width)
    source_grad = jnp.dot(mix_weights.T, tile_flat, precision=lax.Precision.HIGHEST)
    source_grad = source_grad.reshape(NSRC, rows_here, col_width)
    weight_part = jnp.dot(
        tile_flat,
        own_prompts.reshape(NSRC, rows_here * col_width).astype(jnp.float32).T,
        precision=lax.Precision.HIGHEST,
    )
    return (source_grad, weight_part)


def on_device(
    source_prompts,
    task_logits,
    task_ids,
    key_weight,
    value_weight,
    queries,
    keys,
    values,
    cotangent,
):
    col_width = key_weight.shape[1]
    group_examples = task_ids.shape[0]
    mix_weights = jax.nn.softmax(task_logits, axis=1)
    mix_rounded = mix_weights.astype(jnp.bfloat16)
    mixture = jnp.dot(
        mix_rounded,
        source_prompts.reshape(NSRC, PTOK * col_width),
        preferred_element_type=jnp.float32,
    )
    mixture = mixture.astype(jnp.bfloat16).reshape(NTASK, PTOK, col_width)
    pair_weight = jnp.concatenate([key_weight, value_weight], axis=1)
    portion = lax.all_gather(mixture, "mp", axis=2, tiled=True)
    portion_rows = portion.reshape(NTASK * PTOK, portion.shape[2])
    projected = jnp.dot(portion_rows, pair_weight, preferred_element_type=jnp.float32)
    projected = projected.astype(jnp.bfloat16).reshape(NTASK, PTOK, 2, col_width)
    task_range = jnp.arange(NTASK, dtype=jnp.int32)
    selector_all = (task_ids[:, None] == task_range[None, :]).astype(jnp.bfloat16)
    table_full = lax.all_gather(projected, "mp", axis=3, tiled=True)
    own_offset = lax.axis_index("mp") * E_DEV
    own_selector = lax.dynamic_slice_in_dim(selector_all, own_offset, E_DEV, 0)
    chosen = jnp.dot(
        own_selector, table_full.reshape(NTASK, PTOK * 2 * D), preferred_element_type=jnp.float32
    )
    prompt_pair = chosen.astype(jnp.bfloat16).reshape(E_DEV, PTOK, 2, D)
    attended, outgoing_grads = example_block(prompt_pair, queries, keys, values, cotangent)
    incoming = lax.all_to_all(outgoing_grads, "mp", split_axis=3, concat_axis=0, tiled=True)
    group_grads = jnp.dot(
        selector_all.T,
        incoming.reshape(group_examples, PTOK * 2 * col_width),
        preferred_element_type=jnp.float32,
    )
    pair_weight_t = pair_weight.astype(jnp.float32).T
    task_rows = lax.psum_scatter(
        group_grads.reshape(NTASK, PTOK, 2 * col_width), "dp", scatter_dimension=1, tiled=True
    )
    rows_here = task_rows.shape[1]
    row_terms = jnp.dot(
        task_rows.reshape(NTASK * rows_here, 2 * col_width),
        pair_weight_t,
        precision=lax.Precision.HIGHEST,
    ).reshape(NTASK, rows_here, D)
    tile_grad = lax.psum_scatter(row_terms, "mp", scatter_dimension=2, tiled=True)
    source_grad, weight_part = tile_products(tile_grad, source_prompts, mix_weights, col_width)
    weight_grad = lax.psum(weight_part, ("dp", "mp"))
    logits_grad = mix_weights * (
        weight_grad - jnp.sum(mix_weights * weight_grad, axis=1, keepdims=True)
    )
    return (attended, source_grad, logits_grad)


BF = jnp.bfloat16
F32 = jnp.float32


def mm(a, b, ca=1, cb=0, precision=None):
    return lax.dot_general(
        a, b, (((ca,), (cb,)), ((), ())), preferred_element_type=F32, precision=precision
    )


def chain_kernel(
    ndp, nmp,
    logits, ids_in, sp_hbm, kw_hbm, vw_hbm, q_hbm, k_hbm, v_hbm, c_hbm,
    att_hbm, tile_out, lg_out, w_hbm,
    att_out, w_out, p_v, kw_v, vw_v, q_v, k_v, v_v, c_v,
    mixed, ids_own, ids_buf, sbuf, pair, gr, rbuf, ys, yr, zs, zr, wp, wbuf,
    lsem, gs, gv, fs, fv, js, jv, bs, bv, cs, cv, us, uv, ts, tv, ws, wv,
):
    n = ndp * nmp
    nz = nmp // 2
    width = kw_v.shape[1]
    rows = p_v.shape[1]
    nsrc = p_v.shape[0]
    ntask = logits.shape[0]
    tp = ntask * rows
    spn = nsrc * rows
    seq = q_v.shape[0]
    d = lax.axis_index("dp")
    m = lax.axis_index("mp")
    z = m // 2
    y = m % 2
    me = d * nmp + m
    other = z * 2 + (1 - y)

    shift = rows.bit_length() - 1

    def iota(shape, axis):
        return lax.broadcasted_iota(jnp.int32, shape, axis)

    def outer(a):
        return lax.shift_right_logical(a, jnp.int32(shift))

    def same_row(shape):
        return ((iota(shape, 0) ^ iota(shape, 1)) & (rows - 1)) == 0

    def remote(src, dst, ss, rs, dd, mm_):
        return pltpu.make_async_remote_copy(
            src_ref=src, dst_ref=dst, send_sem=ss, recv_sem=rs,
            device_id=(dd, mm_), device_id_type=pl.DeviceIdType.MESH,
        )

    barrier = pltpu.get_barrier_semaphore()

    @pl.loop(1, n)
    def _(k):
        to = lax.rem(me + k, n)
        pl.semaphore_signal(
            barrier, inc=1, device_id=(to // nmp, lax.rem(to, nmp)),
            device_id_type=pl.DeviceIdType.MESH,
        )

    loads = [
        pltpu.make_async_copy(
            sp_hbm.at[:, pl.ds(pl.multiple_of(d * rows, rows), rows), :], p_v, lsem.at[0]
        )
    ]
    for i, (a, b) in enumerate(
        ((kw_hbm, kw_v), (vw_hbm, vw_v), (k_hbm, k_v), (q_hbm, q_v), (v_hbm, v_v), (c_hbm, c_v))
    ):
        loads.append(pltpu.make_async_copy(a, b, lsem.at[1 + i]))
    loads[0].start()

    lg = logits[...]
    ex = jnp.exp(lg - jnp.max(lg, axis=1, keepdims=True))
    mix = ex / jnp.sum(ex, axis=1, keepdims=True)
    up = (
        outer(iota((tp, ntask), 0)) == iota((tp, ntask), 1)
    )
    tall = mm(jnp.where(up, 1.0, 0.0), mix.astype(BF).astype(F32)).astype(BF)
    out = (
        outer(iota((nsrc, spn), 1)) == iota((nsrc, spn), 0)
    )
    wide = mm(tall, jnp.where(out, 1.0, 0.0).astype(BF))
    w_out[...] = jnp.where(same_row((tp, spn)), wide, 0.0).astype(BF)
    for j in range(ids_in.shape[0]):
        line = jnp.full((1, tp), ids_in[j], jnp.int32).astype(F32)
        ids_own[pl.ds(j, 1), :] = line
        ids_buf[d, pl.ds(j, 1), :] = line

    loads[0].wait()
    for c in loads[1:]:
        c.start()
    w_save = pltpu.make_async_copy(w_out, w_hbm, lsem.at[9])
    w_save.start()
    mixed[m] = mm(w_out[...], p_v[...].reshape(spn, width)).astype(BF)

    pl.semaphore_wait(barrier, n - 1)

    idc = []
    for j in range(1, ndp):
        c = remote(ids_own, ids_buf.at[d], js.at[j], jv.at[j], lax.rem(d + j, ndp), m)
        c.start()
        idc.append(c)
    gat = []
    for j in range(1, nz):
        c = remote(
            mixed.at[m], mixed.at[m], gs.at[j], gv.at[j], d, lax.rem(z + j, nz) * 2 + y
        )
        c.start()
        gat.append(c)
    fwd = [remote(mixed.at[m], mixed.at[m], fs.at[0], fv.at[0], d, other)]
    fwd[0].start()
    for c in idc:
        c.wait()
    loads[1].wait()
    loads[2].wait()

    def part(slot):
        block = mixed[slot]
        at = pl.ds(pl.multiple_of(slot * width, width), width)
        return mm(block, kw_v[at, :]), mm(block, vw_v[at, :])

    pk, pv = part(m)
    for j in range(1, nz):
        slot = lax.rem(z + nz - j, nz) * 2 + y
        gat[j - 1].wait_recv()
        c = remote(mixed.at[slot], mixed.at[slot], fs.at[j], fv.at[j], d, other)
        c.start()
        fwd.append(c)
        a, b = part(slot)
        pk, pv = pk + a, pv + b
    for j in range(nz):
        slot = lax.rem(z + nz - j, nz) * 2 + (1 - y)
        fwd[j].wait_recv()
        a, b = part(slot)
        pk, pv = pk + a, pv + b

    ids_all = ids_buf[...].reshape(n, tp).astype(BF)
    rep = (
        outer(iota((n * rows, n), 0)) == iota((n * rows, n), 1)
    )
    ids_x = mm(jnp.where(rep, 1.0, 0.0).astype(BF), ids_all)
    sel = jnp.where(
        (ids_x == outer(iota((n * rows, tp), 1)).astype(F32)) & same_row((n * rows, tp)), 1.0, 0.0
    ).astype(BF)
    sbuf[:, 0] = mm(sel, pk.astype(BF)).astype(BF).reshape(n, rows, width)
    sbuf[:, 1] = mm(sel, pv.astype(BF)).astype(BF).reshape(n, rows, width)

    my_rows = pl.ds(pl.multiple_of(d * rows, rows), rows)
    my_cols = pl.ds(pl.multiple_of(m * width, width), width)

    def b_copy(k):
        dd, gg = lax.rem(k, ndp), k // ndp
        td, tm = lax.rem(d + ndp - dd, ndp), lax.rem(m + nmp - gg, nmp)
        return remote(
            sbuf.at[td * nmp + tm], pair.at[:, my_rows, my_cols], bs.at[k], bv.at[k], td, tm
        )

    own_b = pltpu.make_async_copy(sbuf.at[me], pair.at[:, my_rows, my_cols], lsem.at[7])
    own_b.start()

    @pl.loop(1, n)
    def _(k):
        b_copy(k).start()

    for c in loads[3:]:
        c.wait()
    own_b.wait()

    def c_copy(k):
        dd, gg = lax.rem(k, ndp), k // ndp
        td, tm = lax.rem(d + dd, ndp), lax.rem(m + gg, nmp)
        return remote(
            gr.at[
                :,
                pl.ds(pl.multiple_of(td * rows, rows), rows),
                pl.ds(pl.multiple_of(tm * width, width), width),
            ],
            rbuf.at[me], cs.at[k], cv.at[k], td, tm,
        )

    scale = DH ** (-0.5)
    to_exp2 = scale * 1.4426950408889634
    ptok = pair.shape[1]
    seen = iota((seq, seq), 0) <= iota((seq, seq), 1)

    def group(g, wait_from):
        @pl.loop(wait_from, ndp)
        def _(dd):
            b_copy(g * ndp + dd).wait_recv()

        base = lax.rem(m + g, nmp) * width
        ats, st, gt, va = [], [], [], []
        for h in range(width // DH):
            at = pl.ds(pl.multiple_of(base + h * DH, DH), DH)
            ats.append(at)
            ka = jnp.concatenate([pair[0, :, at], k_v[:, at]], axis=0)
            va.append(jnp.concatenate([pair[1, :, at], v_v[:, at]], axis=0))
            st.append(mm(ka, q_v[:, at], 1, 1))
            gt.append(mm(va[h], c_v[:, at], 1, 1))
        for h in range(width // DH):
            at = ats[h]
            s = st[h] * to_exp2
            s = jnp.concatenate([s[:ptok], jnp.where(seen, s[ptok:], mask_fill)], axis=0)
            e = jnp.exp2(s - jnp.max(s, axis=0, keepdims=True))
            a = e * (1.0 / jnp.sum(e, axis=0, keepdims=True))
            ab = a.astype(BF)
            inner = jnp.sum(a * gt[h], axis=0, keepdims=True)
            gs1 = (a[:ptok] * (gt[h][:ptok] - inner)).astype(BF)
            gr[0, :, at] = (mm(gs1, q_v[:, at]) * scale).astype(BF)
            gr[1, :, at] = mm(ab[:ptok], c_v[:, at]).astype(BF)
            att_out[:, at] = mm(ab, va[h], 0, 0).astype(BF)

    group(0, 1)
    own_c = pltpu.make_async_copy(gr.at[:, my_rows, my_cols], rbuf.at[me], lsem.at[8])
    own_c.start()

    @pl.loop(1, ndp)
    def _(dd):
        c_copy(dd).start()

    @pl.loop(1, nmp)
    def _(g):
        group(g, 0)

        @pl.loop(0, ndp)
        def _(dd):
            c_copy(g * ndp + dd).start()

    own_c.wait()
    att_save = pltpu.make_async_copy(att_out, att_hbm, lsem.at[10])
    att_save.start()

    @pl.loop(1, n)
    def _(k):
        c_copy(k).wait_recv()

    tk = mm(sel, rbuf[:, 0].reshape(n * rows, width), 0, 0).astype(BF)
    tv_ = mm(sel, rbuf[:, 1].reshape(n * rows, width), 0, 0).astype(BF)

    def term(slot):
        at = pl.ds(pl.multiple_of(slot * width, width), width)
        return mm(tk, kw_v[at, :], 1, 1) + mm(tv_, vw_v[at, :], 1, 1)

    yc, zc = [None] * nz, [None] * nz
    order = list(range(1, nz)) + [0]
    for j in order:
        ys[j] = term(lax.rem(z + j, nz) * 2 + (1 - y)).astype(BF)
        yc[j] = remote(ys.at[j], yr.at[j], us.at[j], uv.at[j], d, other)
        yc[j].start()
    for j in order:
        to = lax.rem(z + j, nz) * 2 + y
        mine = term(to)
        yc[j].wait_recv()
        mine = mine + yr[j].astype(F32)
        if j:
            zs[j] = mine.astype(BF)
            zc[j] = remote(zs.at[j], zr.at[j], ts.at[j], tv.at[j], d, to)
            zc[j].start()
    for j in range(1, nz):
        zc[j].wait_recv()
        mine = mine + zr[j].astype(F32)
    tile = mine.astype(BF)
    tile_out[...] = tile

    prod = mm(p_v[...].reshape(spn, width), tile, 1, 1)
    prod = jnp.sum(jnp.where(same_row((spn, tp)), prod, 0.0).reshape(nsrc, rows, tp), axis=1)
    fold = (
        outer(iota((ntask, tp), 1)) == iota((ntask, tp), 0)
    )
    part_w = mm(jnp.where(fold, 1.0, 0.0), prod, 1, 1, lax.Precision.HIGHEST)
    wp[...] = part_w
    wbuf[me] = part_w

    def w_copy(k):
        to = lax.rem(me + k, n)
        return remote(wp, wbuf.at[me], ws.at[k], wv.at[k], to // nmp, lax.rem(to, nmp))

    @pl.loop(1, n)
    def _(k):
        w_copy(k).start()

    w_save.wait()
    att_save.wait()
    for c in gat + fwd + yc + zc[1:]:
        c.wait_send()

    @pl.loop(1, n)
    def _(k):
        b_copy(k).wait_send()
        c_copy(k).wait_send()

    @pl.loop(1, n)
    def _(k):
        w_copy(k).wait()

    wg = jnp.sum(wbuf[...], axis=0)
    lg_out[...] = mix * (wg - jnp.sum(mix * wg, axis=1, keepdims=True))


def source_kernel(w_ref, tile_ref, att_ref, lg_ref, out_ref, att_out, lg_out):
    att_out[...] = att_ref[...]
    lg_out[...] = lg_ref[...]
    got = mm(w_ref[...], tile_ref[...], 0, 0)
    out_ref[...] = got.reshape(out_ref.shape)


def per_device(ndp, nmp, *args):
    source_prompts, task_logits, task_ids, key_weight, value_weight = args[:5]
    queries, keys, values, cotangent = args[5:]
    nsrc, ptok, width = source_prompts.shape
    ntask = task_logits.shape[0]
    ge = task_ids.shape[0]
    rows = ptok // ndp
    if width % DH or nmp % 2 or ge != nmp or ptok % ndp or rows % 16 or rows & (rows - 1) or ntask * rows != 128:
        return on_device(*args)
    n, nz = ndp * nmp, nmp // 2
    tp, spn = ntask * rows, nsrc * rows
    seq, full = queries.shape[1:]
    vmem = pl.BlockSpec(memory_space=pltpu.VMEM)
    hbm = pl.BlockSpec(memory_space=pl.ANY)
    dma = pltpu.SemaphoreType.DMA
    attended, tile, logits_grad, w_big = pl.pallas_call(
        functools.partial(chain_kernel, ndp, nmp),
        out_shape=(
            jax.ShapeDtypeStruct((seq, full), BF),
            jax.ShapeDtypeStruct((tp, width), BF),
            jax.ShapeDtypeStruct((ntask, nsrc), F32),
            jax.ShapeDtypeStruct((tp, spn), BF),
        ),
        in_specs=[vmem, pl.BlockSpec(memory_space=pltpu.SMEM)] + [hbm] * 7,
        out_specs=(hbm, vmem, vmem, hbm),
        scratch_shapes=[
            pltpu.VMEM((seq, full), BF),
            pltpu.VMEM((tp, spn), BF),
            pltpu.VMEM((nsrc, rows, width), BF),
            pltpu.VMEM((full, width), BF),
            pltpu.VMEM((full, width), BF),
            pltpu.VMEM((seq, full), BF),
            pltpu.VMEM((seq, full), BF),
            pltpu.VMEM((seq, full), BF),
            pltpu.VMEM((seq, full), BF),
            pltpu.VMEM((nmp, tp, width), BF),
            pltpu.VMEM((ge, tp), F32),
            pltpu.VMEM((ndp, ge, tp), F32),
            pltpu.VMEM((n, 2, rows, width), BF),
            pltpu.VMEM((2, ptok, full), BF),
            pltpu.VMEM((2, ptok, full), BF),
            pltpu.VMEM((n, 2, rows, width), BF),
            pltpu.VMEM((nz, tp, width), BF),
            pltpu.VMEM((nz, tp, width), BF),
            pltpu.VMEM((nz, tp, width), BF),
            pltpu.VMEM((nz, tp, width), BF),
            pltpu.VMEM((ntask, nsrc), F32),
            pltpu.VMEM((n, ntask, nsrc), F32),
            dma((11,)),
            dma((nz,)), dma((nz,)), dma((nz,)), dma((nz,)),
            dma((ndp,)), dma((ndp,)),
            dma((n,)), dma((n,)), dma((n,)), dma((n,)),
            dma((nz,)), dma((nz,)), dma((nz,)), dma((nz,)),
            dma((n,)), dma((n,)),
        ],
        compiler_params=pltpu.CompilerParams(
            collective_id=0, has_side_effects=True, vmem_limit_bytes=60 * 2**20
        ),
        name="chain",
    )(
        task_logits, task_ids, source_prompts, key_weight, value_weight,
        queries.reshape(seq, full), keys.reshape(seq, full),
        values.reshape(seq, full), cotangent.reshape(seq, full),
    )
    steps = 2
    source_grad, attended, logits_grad = pl.pallas_call(
        source_kernel,
        grid=(steps,),
        out_shape=(
            jax.ShapeDtypeStruct((nsrc, rows, width), F32),
            jax.ShapeDtypeStruct((seq, full), BF),
            jax.ShapeDtypeStruct((ntask, nsrc), F32),
        ),
        in_specs=[
            pl.BlockSpec((tp, spn // steps), lambda i: (0, i)),
            pl.BlockSpec((tp, width), lambda i: (0, 0)),
            pl.BlockSpec((seq // steps, full), lambda i: (i, 0)),
            pl.BlockSpec((ntask, nsrc), lambda i: (0, 0)),
        ],
        out_specs=(
            pl.BlockSpec((nsrc // steps, rows, width), lambda i: (i, 0, 0)),
            pl.BlockSpec((seq // steps, full), lambda i: (i, 0)),
            pl.BlockSpec((ntask, nsrc), lambda i: (0, 0)),
        ),
        name="source_grad",
    )(w_big, tile, attended, logits_grad)
    return (attended.reshape(queries.shape), source_grad, logits_grad)


def solution(mesh):
    placed = (
        P(None, None, "mp"),
        P(),
        P("dp"),
        P(None, "mp"),
        P(None, "mp"),
        P(("dp", "mp"), None, None),
        P(("dp", "mp"), None, None),
        P(("dp", "mp"), None, None),
        P(("dp", "mp"), None, None),
    )
    return jax.shard_map(
        functools.partial(per_device, mesh.shape["dp"], mesh.shape["mp"]),
        mesh=mesh,
        in_specs=placed,
        out_specs=(P(("dp", "mp"), None, None), P(None, "dp", "mp"), P()),
        check_vma=False,
    )
```

```python
import functools

import jax
import jax.numpy as jnp
from jax import lax
from jax.experimental import pallas as pl
from jax.experimental.pallas import tpu as pltpu
from jax.sharding import PartitionSpec as P

D = 4096
HEADS = 32
DH = 128
NSRC = 128
NTASK = 8
PTOK = 64
SEQ = 128
E_DEV = 1


mask_fill = -1e30


def example_block(prompt_pair, queries, keys, values, cotangent):
    examples = queries.shape[0]
    score_scale = DH ** (-0.5)
    key_all = jnp.concatenate([prompt_pair[:, :, 0, :], keys], axis=1)
    value_all = jnp.concatenate([prompt_pair[:, :, 1, :], values], axis=1)
    query_heads = queries.reshape(examples, SEQ, HEADS, DH)
    key_heads = key_all.reshape(examples, PTOK + SEQ, HEADS, DH)
    value_heads = value_all.reshape(examples, PTOK + SEQ, HEADS, DH)
    cot_heads = cotangent.reshape(examples, SEQ, HEADS, DH)
    scores = (
        jnp.einsum("eihd,ejhd->ehij", query_heads, key_heads, preferred_element_type=jnp.float32)
        * score_scale
    )
    column = jnp.arange(PTOK + SEQ)[None, :]
    position = jnp.arange(SEQ)[:, None]
    visible = (column < PTOK) | (column - PTOK <= position)
    scores = jnp.where(visible[None, None], scores, mask_fill)
    top_score = jnp.max(scores, axis=3, keepdims=True)
    exponent = jnp.exp(scores - top_score)
    attention = exponent / jnp.sum(exponent, axis=3, keepdims=True)
    attention_rounded = attention.astype(jnp.bfloat16)
    attended = jnp.einsum(
        "ehij,ejhd->eihd", attention_rounded, value_heads, preferred_element_type=jnp.float32
    )
    attended = attended.astype(jnp.bfloat16).reshape(examples, SEQ, D)
    grad_attention = jnp.einsum(
        "eihd,ejhd->ehij", cot_heads, value_heads, preferred_element_type=jnp.float32
    )
    inner_sum = jnp.sum(attention * grad_attention, axis=3, keepdims=True)
    grad_scores = (attention * (grad_attention - inner_sum)).astype(jnp.bfloat16)
    key_grads = jnp.einsum(
        "ehij,eihd->ejhd",
        grad_scores[:, :, :, :PTOK],
        query_heads,
        preferred_element_type=jnp.float32,
    )
    key_grads = (key_grads * score_scale).astype(jnp.bfloat16).reshape(examples, PTOK, D)
    value_grads = jnp.einsum(
        "ehij,eihd->ejhd",
        attention_rounded[:, :, :, :PTOK],
        cot_heads,
        preferred_element_type=jnp.float32,
    )
    value_grads = value_grads.astype(jnp.bfloat16).reshape(examples, PTOK, D)
    return (attended, jnp.stack([key_grads, value_grads], axis=2))


def tile_products(tile_grad, source_prompts, mix_weights, col_width):
    rows_here = tile_grad.shape[1]
    own_prompts = lax.dynamic_slice_in_dim(
        source_prompts, lax.axis_index("dp") * rows_here, rows_here, 1
    )
    tile_flat = tile_grad.reshape(NTASK, rows_here * col_width)
    source_grad = jnp.dot(mix_weights.T, tile_flat, precision=lax.Precision.HIGHEST)
    source_grad = source_grad.reshape(NSRC, rows_here, col_width)
    weight_part = jnp.dot(
        tile_flat,
        own_prompts.reshape(NSRC, rows_here * col_width).astype(jnp.float32).T,
        precision=lax.Precision.HIGHEST,
    )
    return (source_grad, weight_part)


def on_device(
    source_prompts,
    task_logits,
    task_ids,
    key_weight,
    value_weight,
    queries,
    keys,
    values,
    cotangent,
):
    col_width = key_weight.shape[1]
    group_examples = task_ids.shape[0]
    mix_weights = jax.nn.softmax(task_logits, axis=1)
    mix_rounded = mix_weights.astype(jnp.bfloat16)
    mixture = jnp.dot(
        mix_rounded,
        source_prompts.reshape(NSRC, PTOK * col_width),
        preferred_element_type=jnp.float32,
    )
    mixture = mixture.astype(jnp.bfloat16).reshape(NTASK, PTOK, col_width)
    pair_weight = jnp.concatenate([key_weight, value_weight], axis=1)
    portion = lax.all_gather(mixture, "mp", axis=2, tiled=True)
    portion_rows = portion.reshape(NTASK * PTOK, portion.shape[2])
    projected = jnp.dot(portion_rows, pair_weight, preferred_element_type=jnp.float32)
    projected = projected.astype(jnp.bfloat16).reshape(NTASK, PTOK, 2, col_width)
    task_range = jnp.arange(NTASK, dtype=jnp.int32)
    selector_all = (task_ids[:, None] == task_range[None, :]).astype(jnp.bfloat16)
    table_full = lax.all_gather(projected, "mp", axis=3, tiled=True)
    own_offset = lax.axis_index("mp") * E_DEV
    own_selector = lax.dynamic_slice_in_dim(selector_all, own_offset, E_DEV, 0)
    chosen = jnp.dot(
        own_selector, table_full.reshape(NTASK, PTOK * 2 * D), preferred_element_type=jnp.float32
    )
    prompt_pair = chosen.astype(jnp.bfloat16).reshape(E_DEV, PTOK, 2, D)
    attended, outgoing_grads = example_block(prompt_pair, queries, keys, values, cotangent)
    incoming = lax.all_to_all(outgoing_grads, "mp", split_axis=3, concat_axis=0, tiled=True)
    group_grads = jnp.dot(
        selector_all.T,
        incoming.reshape(group_examples, PTOK * 2 * col_width),
        preferred_element_type=jnp.float32,
    )
    pair_weight_t = pair_weight.astype(jnp.float32).T
    task_rows = lax.psum_scatter(
        group_grads.reshape(NTASK, PTOK, 2 * col_width), "dp", scatter_dimension=1, tiled=True
    )
    rows_here = task_rows.shape[1]
    row_terms = jnp.dot(
        task_rows.reshape(NTASK * rows_here, 2 * col_width),
        pair_weight_t,
        precision=lax.Precision.HIGHEST,
    ).reshape(NTASK, rows_here, D)
    tile_grad = lax.psum_scatter(row_terms, "mp", scatter_dimension=2, tiled=True)
    source_grad, weight_part = tile_products(tile_grad, source_prompts, mix_weights, col_width)
    weight_grad = lax.psum(weight_part, ("dp", "mp"))
    logits_grad = mix_weights * (
        weight_grad - jnp.sum(mix_weights * weight_grad, axis=1, keepdims=True)
    )
    return (attended, source_grad, logits_grad)


BF = jnp.bfloat16
F32 = jnp.float32


def mm(a, b, ca=1, cb=0, precision=None):
    return lax.dot_general(
        a, b, (((ca,), (cb,)), ((), ())), preferred_element_type=F32, precision=precision
    )


def chain_kernel(
    ndp, nmp,
    logits, ids_in, sp_hbm, kw_hbm, vw_hbm, q_hbm, k_hbm, v_hbm, c_hbm,
    att_hbm, tile_out, lg_out, w_hbm,
    att_out, w_out, p_v, kw_v, vw_v, q_v, k_v, v_v, c_v,
    mixed, ids_own, ids_buf, sbuf, pair, gr, rbuf, ys, yr, zs, zr, wp, wbuf,
    lsem, gs, gv, fs, fv, js, jv, bs, bv, cs, cv, us, uv, ts, tv, ws, wv,
):
    n = ndp * nmp
    nz = nmp // 2
    width = kw_v.shape[1]
    rows = p_v.shape[1]
    nsrc = p_v.shape[0]
    ntask = logits.shape[0]
    tp = ntask * rows
    spn = nsrc * rows
    seq = q_v.shape[0]
    d = lax.axis_index("dp")
    m = lax.axis_index("mp")
    z = m // 2
    y = m % 2
    me = d * nmp + m
    other = z * 2 + (1 - y)

    shift = rows.bit_length() - 1

    def iota(shape, axis):
        return lax.broadcasted_iota(jnp.int32, shape, axis)

    def outer(a):
        return lax.shift_right_logical(a, jnp.int32(shift))

    def same_row(shape):
        return ((iota(shape, 0) ^ iota(shape, 1)) & (rows - 1)) == 0

    def remote(src, dst, ss, rs, dd, mm_):
        return pltpu.make_async_remote_copy(
            src_ref=src, dst_ref=dst, send_sem=ss, recv_sem=rs,
            device_id=(dd, mm_), device_id_type=pl.DeviceIdType.MESH,
        )

    barrier = pltpu.get_barrier_semaphore()

    @pl.loop(1, n)
    def _(k):
        to = lax.rem(me + k, n)
        pl.semaphore_signal(
            barrier, inc=1, device_id=(to // nmp, lax.rem(to, nmp)),
            device_id_type=pl.DeviceIdType.MESH,
        )

    loads = [
        pltpu.make_async_copy(
            sp_hbm.at[:, pl.ds(pl.multiple_of(d * rows, rows), rows), :], p_v, lsem.at[0]
        )
    ]
    for i, (a, b) in enumerate(
        ((kw_hbm, kw_v), (vw_hbm, vw_v), (k_hbm, k_v), (q_hbm, q_v), (v_hbm, v_v), (c_hbm, c_v))
    ):
        loads.append(pltpu.make_async_copy(a, b, lsem.at[1 + i]))
    loads[0].start()

    lg = logits[...]
    ex = jnp.exp(lg - jnp.max(lg, axis=1, keepdims=True))
    mix = ex / jnp.sum(ex, axis=1, keepdims=True)
    up = (
        outer(iota((tp, ntask), 0)) == iota((tp, ntask), 1)
    )
    tall = mm(jnp.where(up, 1.0, 0.0), mix.astype(BF).astype(F32)).astype(BF)
    out = (
        outer(iota((nsrc, spn), 1)) == iota((nsrc, spn), 0)
    )
    wide = mm(tall, jnp.where(out, 1.0, 0.0).astype(BF))
    w_out[...] = jnp.where(same_row((tp, spn)), wide, 0.0).astype(BF)
    for j in range(ids_in.shape[0]):
        line = jnp.full((1, tp), ids_in[j], jnp.int32).astype(F32)
        ids_own[pl.ds(j, 1), :] = line
        ids_buf[d, pl.ds(j, 1), :] = line

    loads[0].wait()
    for c in loads[1:]:
        c.start()
    w_save = pltpu.make_async_copy(w_out, w_hbm, lsem.at[9])
    w_save.start()
    mixed[m] = mm(w_out[...], p_v[...].reshape(spn, width)).astype(BF)

    pl.semaphore_wait(barrier, n - 1)

    idc = []
    for j in range(1, ndp):
        c = remote(ids_own, ids_buf.at[d], js.at[j], jv.at[j], lax.rem(d + j, ndp), m)
        c.start()
        idc.append(c)
    gat = []
    for j in range(1, nz):
        c = remote(
            mixed.at[m], mixed.at[m], gs.at[j], gv.at[j], d, lax.rem(z + j, nz) * 2 + y
        )
        c.start()
        gat.append(c)
    fwd = [remote(mixed.at[m], mixed.at[m], fs.at[0], fv.at[0], d, other)]
    fwd[0].start()
    for c in idc:
        c.wait()
    loads[1].wait()
    loads[2].wait()

    def part(slot):
        block = mixed[slot]
        at = pl.ds(pl.multiple_of(slot * width, width), width)
        return mm(block, kw_v[at, :]), mm(block, vw_v[at, :])

    pk, pv = part(m)
    for j in range(1, nz):
        slot = lax.rem(z + nz - j, nz) * 2 + y
        gat[j - 1].wait_recv()
        c = remote(mixed.at[slot], mixed.at[slot], fs.at[j], fv.at[j], d, other)
        c.start()
        fwd.append(c)
        a, b = part(slot)
        pk, pv = pk + a, pv + b
    for j in range(nz):
        slot = lax.rem(z + nz - j, nz) * 2 + (1 - y)
        fwd[j].wait_recv()
        a, b = part(slot)
        pk, pv = pk + a, pv + b

    ids_all = ids_buf[...].reshape(n, tp).astype(BF)
    rep = (
        outer(iota((n * rows, n), 0)) == iota((n * rows, n), 1)
    )
    ids_x = mm(jnp.where(rep, 1.0, 0.0).astype(BF), ids_all)
    sel = jnp.where(
        (ids_x == outer(iota((n * rows, tp), 1)).astype(F32)) & same_row((n * rows, tp)), 1.0, 0.0
    ).astype(BF)
    sbuf[:, 0] = mm(sel, pk.astype(BF)).astype(BF).reshape(n, rows, width)
    sbuf[:, 1] = mm(sel, pv.astype(BF)).astype(BF).reshape(n, rows, width)

    my_rows = pl.ds(pl.multiple_of(d * rows, rows), rows)
    my_cols = pl.ds(pl.multiple_of(m * width, width), width)

    def b_copy(k):
        dd, gg = lax.rem(k, ndp), k // ndp
        td, tm = lax.rem(d + ndp - dd, ndp), lax.rem(m + nmp - gg, nmp)
        return remote(
            sbuf.at[td * nmp + tm], pair.at[:, my_rows, my_cols], bs.at[k], bv.at[k], td, tm
        )

    own_b = pltpu.make_async_copy(sbuf.at[me], pair.at[:, my_rows, my_cols], lsem.at[7])
    own_b.start()

    def turn(t):
        return lax.rem(t + nmp // 2 - 1 + t // (nmp // 2 + 1), nmp)

    @pl.loop(1, nmp)
    def _(t):
        @pl.loop(0, ndp)
        def _(dd):
            b_copy(turn(t) * ndp + dd).start()

    @pl.loop(1, ndp)
    def _(dd):
        b_copy(dd).start()

    for c in loads[3:]:
        c.wait()
    own_b.wait()

    def c_copy(k):
        dd, gg = lax.rem(k, ndp), k // ndp
        td, tm = lax.rem(d + dd, ndp), lax.rem(m + gg, nmp)
        return remote(
            gr.at[
                :,
                pl.ds(pl.multiple_of(td * rows, rows), rows),
                pl.ds(pl.multiple_of(tm * width, width), width),
            ],
            rbuf.at[me], cs.at[k], cv.at[k], td, tm,
        )

    scale = DH ** (-0.5)
    to_exp2 = scale * 1.4426950408889634
    ptok = pair.shape[1]
    seen = iota((seq, seq), 0) <= iota((seq, seq), 1)

    def group(g, wait_from):
        @pl.loop(wait_from, ndp)
        def _(dd):
            b_copy(g * ndp + dd).wait_recv()

        base = lax.rem(m + g, nmp) * width
        ats, st, gt, va = [], [], [], []
        for h in range(width // DH):
            at = pl.ds(pl.multiple_of(base + h * DH, DH), DH)
            ats.append(at)
            ka = jnp.concatenate([pair[0, :, at], k_v[:, at]], axis=0)
            va.append(jnp.concatenate([pair[1, :, at], v_v[:, at]], axis=0))
            st.append(mm(ka, q_v[:, at], 1, 1))
            gt.append(mm(va[h], c_v[:, at], 1, 1))
        for h in range(width // DH):
            at = ats[h]
            s = st[h] * to_exp2
            s = jnp.concatenate([s[:ptok], jnp.where(seen, s[ptok:], mask_fill)], axis=0)
            e = jnp.exp2(s - jnp.max(s, axis=0, keepdims=True))
            a = e * (1.0 / jnp.sum(e, axis=0, keepdims=True))
            ab = a.astype(BF)
            inner = jnp.sum(a * gt[h], axis=0, keepdims=True)
            gs1 = (a[:ptok] * (gt[h][:ptok] - inner)).astype(BF)
            gr[0, :, at] = (mm(gs1, q_v[:, at]) * scale).astype(BF)
            gr[1, :, at] = mm(ab[:ptok], c_v[:, at]).astype(BF)
            att_out[:, at] = mm(ab, va[h], 0, 0).astype(BF)

    group(0, 1)
    own_c = pltpu.make_async_copy(gr.at[:, my_rows, my_cols], rbuf.at[me], lsem.at[8])
    own_c.start()

    @pl.loop(1, ndp)
    def _(dd):
        c_copy(dd).start()

    @pl.loop(1, nmp)
    def _(t):
        g = turn(t)
        group(g, 0)

        @pl.loop(0, ndp)
        def _(dd):
            c_copy(g * ndp + dd).start()

    own_c.wait()
    att_save = pltpu.make_async_copy(att_out, att_hbm, lsem.at[10])
    att_save.start()

    @pl.loop(1, n)
    def _(k):
        c_copy(k).wait_recv()

    tk = mm(sel, rbuf[:, 0].reshape(n * rows, width), 0, 0).astype(BF)
    tv_ = mm(sel, rbuf[:, 1].reshape(n * rows, width), 0, 0).astype(BF)

    def term(slot):
        at = pl.ds(pl.multiple_of(slot * width, width), width)
        return mm(tk, kw_v[at, :], 1, 1) + mm(tv_, vw_v[at, :], 1, 1)

    yc, zc = [None] * nz, [None] * nz
    order = list(range(1, nz)) + [0]
    for j in order:
        ys[j] = term(lax.rem(z + j, nz) * 2 + (1 - y)).astype(BF)
        yc[j] = remote(ys.at[j], yr.at[j], us.at[j], uv.at[j], d, other)
        yc[j].start()
    for j in order:
        to = lax.rem(z + j, nz) * 2 + y
        mine = term(to)
        yc[j].wait_recv()
        mine = mine + yr[j].astype(F32)
        if j:
            zs[j] = mine.astype(BF)
            zc[j] = remote(zs.at[j], zr.at[j], ts.at[j], tv.at[j], d, to)
            zc[j].start()
    for j in range(1, nz):
        zc[j].wait_recv()
        mine = mine + zr[j].astype(F32)
    tile = mine.astype(BF)
    tile_out[...] = tile

    prod = mm(p_v[...].reshape(spn, width), tile, 1, 1)
    prod = jnp.sum(jnp.where(same_row((spn, tp)), prod, 0.0).reshape(nsrc, rows, tp), axis=1)
    fold = (
        outer(iota((ntask, tp), 1)) == iota((ntask, tp), 0)
    )
    part_w = mm(jnp.where(fold, 1.0, 0.0), prod, 1, 1, lax.Precision.HIGHEST)
    wp[...] = part_w
    wbuf[me] = part_w

    def w_copy(k):
        to = lax.rem(me + k, n)
        return remote(wp, wbuf.at[me], ws.at[k], wv.at[k], to // nmp, lax.rem(to, nmp))

    @pl.loop(1, n)
    def _(k):
        w_copy(k).start()

    w_save.wait()
    att_save.wait()
    for c in gat + fwd + yc + zc[1:]:
        c.wait_send()

    @pl.loop(1, n)
    def _(k):
        b_copy(k).wait_send()
        c_copy(k).wait_send()

    @pl.loop(1, n)
    def _(k):
        w_copy(k).wait()

    wg = jnp.sum(wbuf[...], axis=0)
    lg_out[...] = mix * (wg - jnp.sum(mix * wg, axis=1, keepdims=True))


def source_kernel(w_ref, tile_ref, att_ref, lg_ref, out_ref, att_out, lg_out):
    att_out[...] = att_ref[...]
    lg_out[...] = lg_ref[...]
    got = mm(w_ref[...], tile_ref[...], 0, 0)
    out_ref[...] = got.reshape(out_ref.shape)


def per_device(ndp, nmp, *args):
    source_prompts, task_logits, task_ids, key_weight, value_weight = args[:5]
    queries, keys, values, cotangent = args[5:]
    nsrc, ptok, width = source_prompts.shape
    ntask = task_logits.shape[0]
    ge = task_ids.shape[0]
    rows = ptok // ndp
    if width % DH or nmp % 4 or ge != nmp or ptok % ndp or rows % 16 or rows & (rows - 1) or ntask * rows != 128:
        return on_device(*args)
    n, nz = ndp * nmp, nmp // 2
    tp, spn = ntask * rows, nsrc * rows
    seq, full = queries.shape[1:]
    vmem = pl.BlockSpec(memory_space=pltpu.VMEM)
    hbm = pl.BlockSpec(memory_space=pl.ANY)
    dma = pltpu.SemaphoreType.DMA
    attended, tile, logits_grad, w_big = pl.pallas_call(
        functools.partial(chain_kernel, ndp, nmp),
        out_shape=(
            jax.ShapeDtypeStruct((seq, full), BF),
            jax.ShapeDtypeStruct((tp, width), BF),
            jax.ShapeDtypeStruct((ntask, nsrc), F32),
            jax.ShapeDtypeStruct((tp, spn), BF),
        ),
        in_specs=[vmem, pl.BlockSpec(memory_space=pltpu.SMEM)] + [hbm] * 7,
        out_specs=(hbm, vmem, vmem, hbm),
        scratch_shapes=[
            pltpu.VMEM((seq, full), BF),
            pltpu.VMEM((tp, spn), BF),
            pltpu.VMEM((nsrc, rows, width), BF),
            pltpu.VMEM((full, width), BF),
            pltpu.VMEM((full, width), BF),
            pltpu.VMEM((seq, full), BF),
            pltpu.VMEM((seq, full), BF),
            pltpu.VMEM((seq, full), BF),
            pltpu.VMEM((seq, full), BF),
            pltpu.VMEM((nmp, tp, width), BF),
            pltpu.VMEM((ge, tp), F32),
            pltpu.VMEM((ndp, ge, tp), F32),
            pltpu.VMEM((n, 2, rows, width), BF),
            pltpu.VMEM((2, ptok, full), BF),
            pltpu.VMEM((2, ptok, full), BF),
            pltpu.VMEM((n, 2, rows, width), BF),
            pltpu.VMEM((nz, tp, width), BF),
            pltpu.VMEM((nz, tp, width), BF),
            pltpu.VMEM((nz, tp, width), BF),
            pltpu.VMEM((nz, tp, width), BF),
            pltpu.VMEM((ntask, nsrc), F32),
            pltpu.VMEM((n, ntask, nsrc), F32),
            dma((11,)),
            dma((nz,)), dma((nz,)), dma((nz,)), dma((nz,)),
            dma((ndp,)), dma((ndp,)),
            dma((n,)), dma((n,)), dma((n,)), dma((n,)),
            dma((nz,)), dma((nz,)), dma((nz,)), dma((nz,)),
            dma((n,)), dma((n,)),
        ],
        compiler_params=pltpu.CompilerParams(
            collective_id=0, has_side_effects=True, vmem_limit_bytes=60 * 2**20
        ),
        name="chain",
    )(
        task_logits, task_ids, source_prompts, key_weight, value_weight,
        queries.reshape(seq, full), keys.reshape(seq, full),
        values.reshape(seq, full), cotangent.reshape(seq, full),
    )
    steps = 2
    source_grad, attended, logits_grad = pl.pallas_call(
        source_kernel,
        grid=(steps,),
        out_shape=(
            jax.ShapeDtypeStruct((nsrc, rows, width), F32),
            jax.ShapeDtypeStruct((seq, full), BF),
            jax.ShapeDtypeStruct((ntask, nsrc), F32),
        ),
        in_specs=[
            pl.BlockSpec((tp, spn // steps), lambda i: (0, i)),
            pl.BlockSpec((tp, width), lambda i: (0, 0)),
            pl.BlockSpec((seq // steps, full), lambda i: (i, 0)),
            pl.BlockSpec((ntask, nsrc), lambda i: (0, 0)),
        ],
        out_specs=(
            pl.BlockSpec((nsrc // steps, rows, width), lambda i: (i, 0, 0)),
            pl.BlockSpec((seq // steps, full), lambda i: (i, 0)),
            pl.BlockSpec((ntask, nsrc), lambda i: (0, 0)),
        ),
        name="source_grad",
    )(w_big, tile, attended, logits_grad)
    return (attended.reshape(queries.shape), source_grad, logits_grad)


def solution(mesh):
    placed = (
        P(None, None, "mp"),
        P(),
        P("dp"),
        P(None, "mp"),
        P(None, "mp"),
        P(("dp", "mp"), None, None),
        P(("dp", "mp"), None, None),
        P(("dp", "mp"), None, None),
        P(("dp", "mp"), None, None),
    )
    return jax.shard_map(
        functools.partial(per_device, mesh.shape["dp"], mesh.shape["mp"]),
        mesh=mesh,
        in_specs=placed,
        out_specs=(P(("dp", "mp"), None, None), P(None, "dp", "mp"), P()),
        check_vma=False,
    )
```
